256 devices in a mesh: dp: 16 (over y, x), section: 8 (over z), mp: 2 (over core).
Axes of the slice: x: 4, y: 4, z: 8, core: 2. Of those that a mesh axis runs over, the one named last changes fastest.
Arguments:
- hidden: bfloat16 [128, 32, 3072], P('dp', None, 'mp'), may hold values from -6 to 6
- lengths: int32 [128], P('dp'), may hold values from 1 to 32, as said below
- dest_group: int32 [128], P('dp'), may hold values from 0 to 15, as said below
- w_query: bfloat16 [8, 3072, 3072], P('section', 'dp', 'mp')
- w_keyval: bfloat16 [8, 3072, 2, 2, 128], P('section', None, 'mp')
- w_output: bfloat16 [8, 3072, 3072], P('section', 'dp', 'mp'), may hold values from -0.109375 to 0.109375
- norm_gain: float32 [8, 3072], P('section'), may hold values from 0.5 to 1.5
- norm_bias: float32 [8, 3072], P('section'), may hold values from -3 to 3
Outputs:
- final_rows: bfloat16 [256, 32, 3072], P(('dp', 'section'), None, 'mp')
The draws below stay inside these ranges and needn't reach their ends.
Inputs may be any that keep to these rules, and one draw needn't show every extreme that they name: `lengths`: some file has exactly 32 tokens. `dest_group`: a quarter of the groups receive 16 files, a quarter 16 // 2 and the rest 16 // 4; at most 2 files of one source shard (its 8 files in a row) go to one group, and some shard sends exactly 2 to one group.
All inputs are finite; a program needn't handle non-finite values.
Results may differ from the reference program's by a relative error of at most 0.025.
Values may be sent and summed in bfloat16 or wider, within the bound.
A program may use at most 128 MiB of HBM per device.

```python
import jax
import jax.numpy as jnp
from jax import lax

D = 3072
HEADS = 24
KV_HEADS = 2
HEAD_DIM = 128
LEN = 32
GSLOTS = 16
SRC_FILES = 8
FILES = 128
LAYERS = 8
N_DP = 16
N_MP = 2


def draw_lengths(key, part):
    first_key, second_key = jax.random.split(key)
    values = jax.random.randint(first_key, (FILES,), 1, LEN + 1)
    chosen_spot = jax.random.randint(second_key, (), 0, FILES)
    return jnp.where(jnp.arange(FILES) == chosen_spot, LEN, values).astype(jnp.int32)


def draw_dest_group(key, part):
    key_rank, key_source, key_within = jax.random.split(key, 3)
    ranked = jax.random.permutation(key_rank, N_DP)
    region_first = N_DP * (GSLOTS // 4)
    region_second = N_DP // 2 * (GSLOTS // 4)
    spots = jnp.arange(FILES)
    rank_at = jnp.where(spots < region_first, spots % N_DP, jnp.where(spots < region_first + region_second, (spots - region_first) % (N_DP // 2), (spots - region_first - region_second) % (N_DP // 4)))
    group_at = ranked[rank_at]
    run_order = jax.random.permutation(key_source, N_DP)
    within = jax.vmap(lambda subkey: jax.random.permutation(subkey, SRC_FILES))(jax.random.split(key_within, N_DP))
    target = run_order[:, None] * SRC_FILES + within
    return group_at[target.reshape(-1)].astype(jnp.int32)


def key_columns(key):
    base_key = jax.random.fold_in(key, 7)
    return jax.random.normal(base_key, (LAYERS, D, KV_HEADS, 2, HEAD_DIM), jnp.float32) * D ** (-0.5)


def draw_w_keyval(key, part):
    return key_columns(key).astype(jnp.bfloat16)


def draw_w_query(key, part):
    drawn = jax.random.normal(jax.random.fold_in(key, 11), (LAYERS, D, HEADS, HEAD_DIM), jnp.float32) * D ** (-0.5)
    return drawn.reshape(LAYERS, D, HEADS * HEAD_DIM).astype(jnp.bfloat16)


def block_scale(rng, dims, pieces, smallest, largest):
    level, own = 1.0, jax.random.fold_in(rng, 6)
    for axis_at, parts in pieces:
        draws = jnp.exp(jax.random.uniform(jax.random.fold_in(own, axis_at), (parts,), jnp.float32, smallest / len(pieces), largest / len(pieces)))
        level = level * jnp.repeat(draws, dims[axis_at] // parts).reshape([-1 if axis == axis_at else 1 for axis in range(len(dims))])
    return level


def noise(key, extent, scale, bound, cuts=(), kind=jnp.bfloat16):
    drawn = scale * jax.random.normal(key, extent, jnp.float32)
    if cuts:
        drawn = drawn * block_scale(key, extent, cuts, -0.22, 0.18)
    return jnp.clip(drawn, -bound, bound).astype(kind)


def setup_inputs(seed: int = 0) -> dict:
    arg_keys = jax.random.split(jax.random.key(seed), 9)
    return {
        "hidden": noise(arg_keys[0], (FILES, LEN, D), 1.0, 6.0, ((0, 16), (2, 2))),
        "lengths": draw_lengths(jax.random.fold_in(arg_keys[8], 71), 0),
        "dest_group": draw_dest_group(jax.random.fold_in(arg_keys[8], 71), 0),
        "w_query": draw_w_query(jax.random.fold_in(arg_keys[8], 71), 0),
        "w_keyval": draw_w_keyval(jax.random.fold_in(arg_keys[8], 71), 0),
        "w_output": noise(arg_keys[5], (LAYERS, D, HEADS * HEAD_DIM), (HEADS * HEAD_DIM) ** -0.5, 0.109375, ((0, 8), (1, 16), (2, 2))),
        "norm_gain": jnp.clip(1.0 + 0.1 * jax.random.normal(arg_keys[6], (LAYERS, D), jnp.float32), 0.5, 1.5),
        "norm_bias": noise(arg_keys[7], (LAYERS, D), 0.5, 3.0, ((0, 8),), jnp.float32),
    }


rope_base = 100000.0
norm_eps = 1e-05

def rope_tables(length_n, head_size):
    position = jnp.arange(length_n).astype(jnp.float32)
    fraction = jnp.arange(head_size // 2).astype(jnp.float32) * (2.0 / head_size)
    inverse = jnp.power(jnp.float32(rope_base), -fraction)
    angles = position[:, None] * inverse[None, :]
    angles = jnp.concatenate([angles, angles], axis=-1)
    return (jnp.cos(angles), jnp.sin(angles))

def rotate_heads(values, cosine, sine):
    half_size = values.shape[-1] // 2
    turned = jnp.concatenate([-values[..., half_size:], values[..., :half_size]], axis=-1)
    return values * cosine + turned * sine

def layer_norm(stream, gain_row, bias_row):
    values = stream.astype(jnp.float32)
    center = lax.optimization_barrier(jnp.mean(values, axis=-1, keepdims=True))
    spread = lax.optimization_barrier(jnp.mean(jnp.square(values - center), axis=-1, keepdims=True))
    scaled = (values - center) * lax.rsqrt(spread + norm_eps)
    return (scaled * gain_row.astype(jnp.float32) + bias_row.astype(jnp.float32)).astype(jnp.bfloat16)

def attend(query_all, key_all, value_all, file_lengths, score_scale):
    scores = jnp.einsum('pikgh,pjkh->pkgij', query_all.astype(jnp.float32), key_all.astype(jnp.float32)) * score_scale
    length_n = scores.shape[-1]
    row_pos = jnp.arange(length_n)[:, None]
    col_pos = jnp.arange(length_n)[None, :]
    causal = (col_pos <= row_pos)[None, None, None, :, :]
    inside = col_pos[None, None, None, :, :] < file_lengths[:, None, None, None, None]
    scores = jnp.where(causal & inside, scores, -jnp.inf)
    highest = lax.optimization_barrier(jnp.max(scores, axis=-1, keepdims=True))
    weights = jnp.exp(scores - highest)
    probs = (weights / lax.optimization_barrier(jnp.sum(weights, axis=-1, keepdims=True))).astype(jnp.bfloat16)
    context = jnp.einsum('pkgij,pjkh->pikgh', probs.astype(jnp.float32), value_all.astype(jnp.float32))
    return context.astype(jnp.bfloat16)

def apply_layer(stream, file_lengths, query_w, keyval_w, output_w, gain_row, bias_row, cosine, sine):
    files_n, length_n, model_width = stream.shape
    groups_n = HEADS // KV_HEADS
    normed = layer_norm(stream, gain_row, bias_row).reshape(files_n * length_n, model_width)
    query_all = jnp.dot(normed, query_w, preferred_element_type=jnp.float32)
    query_all = query_all.reshape(files_n, length_n, KV_HEADS, groups_n, HEAD_DIM)
    query_all = rotate_heads(query_all, cosine[None, :, None, None, :], sine[None, :, None, None, :]).astype(jnp.bfloat16)
    keyval = jnp.dot(normed, keyval_w.reshape(model_width, KV_HEADS * 2 * HEAD_DIM), preferred_element_type=jnp.float32)
    keyval = keyval.reshape(files_n, length_n, KV_HEADS, 2, HEAD_DIM)
    key_all = rotate_heads(keyval[:, :, :, 0, :], cosine[None, :, None, :], sine[None, :, None, :]).astype(jnp.bfloat16)
    value_all = keyval[:, :, :, 1, :].astype(jnp.bfloat16)
    context = attend(query_all, key_all, value_all, file_lengths, HEAD_DIM ** (-0.5))
    context = context.reshape(files_n * length_n, HEADS * HEAD_DIM)
    head_cols = HEADS * HEAD_DIM // N_MP
    summed = jnp.zeros((files_n * length_n, model_width), jnp.float32)
    for member in range(N_MP):
        portion = lax.dot_general(context[:, member * head_cols:(member + 1) * head_cols], output_w[:, member * head_cols:(member + 1) * head_cols], (((1,), (1,)), ((), ())), preferred_element_type=jnp.float32)
        portion = lax.optimization_barrier(portion.astype(jnp.bfloat16)).astype(jnp.float32)
        summed = summed + portion
    summed = summed.reshape(files_n, length_n, model_width)
    return (stream.astype(jnp.float32) + summed).astype(jnp.bfloat16)

def reference(hidden, lengths, dest_group, w_query, w_keyval, w_output, norm_gain, norm_bias):
    cosine, sine = rope_tables(LEN, HEAD_DIM)
    stream = hidden
    for layer_idx in range(LAYERS):
        stream = apply_layer(stream, lengths, w_query[layer_idx], w_keyval[layer_idx], w_output[layer_idx], norm_gain[layer_idx], norm_bias[layer_idx], cosine, sine)
    positions = jnp.arange(LEN)
    keep = positions[None, :] < lengths[:, None]
    stream = jnp.where(keep[:, :, None], stream, jnp.zeros_like(stream))
    order = jnp.arange(FILES)
    earlier = (dest_group[None, :] == dest_group[:, None]) & (order[None, :] < order[:, None])
    slot_rank = lax.optimization_barrier(jnp.sum(earlier.astype(jnp.int32), axis=1)).astype(jnp.int32)
    placed = jnp.zeros((N_DP, GSLOTS, LEN, D), jnp.bfloat16)
    placed = placed.at[dest_group.astype(jnp.int32), slot_rank].set(stream)
    return placed.reshape(N_DP * GSLOTS, LEN, D)
```

```python
import functools

import jax
import jax.numpy as jnp
from jax import lax
from jax.experimental import pallas as pl
from jax.experimental.pallas import tpu as pltpu
from jax.sharding import PartitionSpec as P

GSLOTS = 16
MESH = pl.DeviceIdType.MESH

rope_base = 100000.0
norm_eps = 1e-05

FILES_N = 8
LEN = 32
ROWS = FILES_N * LEN
WIDTH = 3072
HALF = 1536
SHARD = 192
PART = 48
HEAD = 128
GROUP = 12
MICRO = 64
MICROS = ROWS // MICRO
MFILES = MICRO // LEN
SECTIONS = 8
SIDE = 4
CUT = 384


def rope_tables(length_n, head_size):
    position = jnp.arange(length_n).astype(jnp.float32)
    fraction = jnp.arange(head_size // 2).astype(jnp.float32) * (2.0 / head_size)
    inverse = jnp.power(jnp.float32(rope_base), -fraction)
    angles = position[:, None] * inverse[None, :]
    cosine, sine = jnp.cos(angles), jnp.sin(angles)
    return (
        jnp.concatenate([cosine, cosine], axis=-1),
        jnp.concatenate([-sine, sine], axis=-1),
    )


def layer_pipeline(
    hidden, wq_own, wo_own, wkv_hbm, gain, bias, cosine, sine, keyok, rowok, out,
    wq, wo, wkv, stream, psend, precv, updated, final, piece, normed, queries, context,
    local_sem, gsend, grecv, zsend, zrecv, asend, arecv, rsend, rrecv, ssend, srecv,
):
    dp = lax.axis_index("dp")
    section = lax.axis_index("section")
    core = lax.axis_index("mp")
    x = lax.rem(dp, SIDE)
    y = dp // SIDE

    def at_xy(xx, yy):
        return lax.rem(yy + SIDE, SIDE) * SIDE + lax.rem(xx + SIDE, SIDE)

    other = 1 - core
    partner = (dp, section, other)
    steps = ((1, 0), (-1, 0), (0, 1), (0, -1))

    barrier = pltpu.get_barrier_semaphore()
    for sx, sy in steps:
        pl.semaphore_signal(
            barrier, inc=1, device_id=(at_xy(x + sx, y + sy), section, core), device_id_type=MESH
        )
    pl.semaphore_signal(barrier, inc=1, device_id=partner, device_id_type=MESH)
    for k in range(1, SECTIONS):
        pl.semaphore_signal(
            barrier, inc=1, device_id=(dp, lax.rem(section + k, SECTIONS), core), device_id_type=MESH
        )
    pl.semaphore_wait(barrier, 4 + 1 + SECTIONS - 1)

    own_cols = pl.ds(pl.multiple_of(core * HALF, HALF), HALF)

    copies = [
        pltpu.make_async_copy(wq_own, wq.at[pl.ds(pl.multiple_of(dp * SHARD, SHARD), SHARD), :], local_sem.at[0]),
        pltpu.make_async_copy(wo_own, wo.at[pl.ds(pl.multiple_of(dp * SHARD, SHARD), SHARD), :], local_sem.at[1]),
        pltpu.make_async_copy(wkv_hbm, wkv, local_sem.at[2]),
    ]
    for copy in copies:
        copy.start()

    def rows_of(source, part):
        return pl.ds(pl.multiple_of(source * SHARD + part * PART, PART), PART)

    def push(w, source, part, direction, own):
        full = (wq, wo)[w]
        sx, sy = steps[direction]
        place = full.at[rows_of(source, part), :]
        src = (wq_own, wo_own)[w].at[pl.ds(part * PART, PART), :] if own else place
        pltpu.make_async_remote_copy(
            src_ref=src,
            dst_ref=place,
            send_sem=gsend.at[w, direction],
            recv_sem=grecv.at[w, source, part],
            device_id=(at_xy(x + sx, y + sy), section, core),
            device_id_type=MESH,
        ).start()

    def arrived(w, source, part):
        place = (wq, wo)[w].at[rows_of(source, part), :]
        pltpu.make_async_copy(place, place, grecv.at[w, source, part]).wait()

    def first_dirs(colour):
        return (0, 1) if colour == 0 else (2, 3)

    def second_dirs(colour):
        return (2, 3) if colour == 0 else (0, 1)

    def along(colour, k):
        return at_xy(x + k, y) if colour == 0 else at_xy(x, y + k)

    def across(colour, k, j):
        return at_xy(x + k, y + j) if colour == 0 else at_xy(x + j, y + k)

    def spread_own(w):
        for dirs in (first_dirs, second_dirs):
            for part in range(2):
                for colour in range(2):
                    for direction in dirs(colour):
                        push(w, dp, 2 * colour + part, direction, True)

    def relay_first(w):
        for part in range(2):
            for colour in range(2):
                forward, backward = first_dirs(colour)
                arrived(w, along(colour, -1), 2 * colour + part)
                if part == 0:
                    push(w, along(colour, -1), 2 * colour, forward, False)
                arrived(w, along(colour, 1), 2 * colour + part)
                if part == 1:
                    push(w, along(colour, 1), 2 * colour + 1, backward, False)
        for k in (-1, 1):
            for part in range(2):
                for colour in range(2):
                    for direction in second_dirs(colour):
                        push(w, along(colour, k), 2 * colour + part, direction, False)

    def relay_opposite(w):
        for part in range(2):
            for colour in range(2):
                arrived(w, along(colour, 2), 2 * colour + part)
                for direction in second_dirs(colour):
                    push(w, along(colour, 2), 2 * colour + part, direction, False)

    def relay_second(w, k):
        for part in range(2):
            for colour in range(2):
                forward, backward = second_dirs(colour)
                arrived(w, across(colour, k, -1), 2 * colour + part)
                if part == 0:
                    push(w, across(colour, k, -1), 2 * colour, forward, False)
                arrived(w, across(colour, k, 1), 2 * colour + part)
                if part == 1:
                    push(w, across(colour, k, 1), 2 * colour + 1, backward, False)

    def finish(w):
        for k in (0, -1, 1, 2):
            for part in range(2):
                for colour in range(2):
                    arrived(w, across(colour, k, 2), 2 * colour + part)

    spread_own(0)
    relay_first(0)
    spread_own(1)
    relay_opposite(0)
    relay_second(0, 0)
    relay_first(1)
    relay_second(0, -1)
    relay_second(0, 1)
    relay_opposite(1)
    relay_second(0, 2)
    finish(0)
    for k in (0, -1, 1, 2):
        relay_second(1, k)
    finish(1)
    for w in range(2):
        for direction in range(4):
            sent = (wq, wo)[w].at[pl.ds(0, 15 * PART), :]
            pltpu.make_async_copy(sent, sent, gsend.at[w, direction]).wait()
    for copy in copies:
        copy.wait()

    @pl.when(section == 0)
    def _():
        first = pltpu.make_async_copy(hidden, stream.at[:, own_cols], local_sem.at[3])
        first.start()
        first.wait()

    row_id = lax.broadcasted_iota(jnp.int32, (MICRO, MICRO), 0)
    col_id = lax.broadcasted_iota(jnp.int32, (MICRO, MICRO), 1)
    causal = (row_id // LEN == col_id // LEN) & (col_id <= row_id)

    def micro_rows(i):
        return pl.ds(pl.multiple_of(i * MICRO, MICRO), MICRO)

    def hop(i, to_section):
        rows = micro_rows(i)
        return pltpu.make_async_remote_copy(
            src_ref=updated.at[rows, :],
            dst_ref=stream.at[rows, own_cols],
            send_sem=zsend.at[i],
            recv_sem=zrecv.at[i],
            device_id=(dp, to_section, core),
            device_id_type=MESH,
        )

    def swap(i):
        rows = micro_rows(i)
        return pltpu.make_async_remote_copy(
            src_ref=stream.at[rows, own_cols],
            dst_ref=stream.at[rows, own_cols],
            send_sem=asend.at[i],
            recv_sem=arecv.at[i],
            device_id=partner,
            device_id_type=MESH,
        )

    def give(i):
        rows = micro_rows(i)
        return pltpu.make_async_remote_copy(
            src_ref=psend.at[rows, :],
            dst_ref=precv.at[rows, :],
            send_sem=rsend.at[i],
            recv_sem=rrecv.at[i],
            device_id=partner,
            device_id_type=MESH,
        )

    def spread(i, target):
        files = pl.ds(i * MFILES, MFILES)
        return (
            final.at[files, target // 4, :, pl.ds((target % 4) * CUT, CUT)],
            piece.at[files, :, :],
        )

    score_scale = HEAD ** (-0.5)

    def step(i, carry):
        rows = micro_rows(i)

        @pl.when(section > 0)
        def _():
            hop(i, section).wait_recv()

        exchange = swap(i)
        exchange.start()
        exchange.wait_recv()

        for block in range(MICRO // 16):
            part = pl.ds(pl.multiple_of(i * MICRO + block * 16, 16), 16)
            values = stream[part, :].astype(jnp.float32)
            center = jnp.mean(values, axis=-1, keepdims=True)
            values = values - center
            variance = jnp.mean(values * values, axis=-1, keepdims=True)
            scaled = values * lax.rsqrt(variance + norm_eps)
            normed[block * 16 : (block + 1) * 16, :] = (scaled * gain[...] + bias[...]).astype(
                jnp.bfloat16
            )

        cos_t = cosine[...]
        sin_t = sine[...]

        def rotate(values):
            return values * cos_t + pltpu.roll(values, HEAD // 2, 1) * sin_t

        keyval = jnp.dot(normed[...], wkv[...], preferred_element_type=jnp.float32)
        key = rotate(keyval[:, :HEAD]).astype(jnp.bfloat16)
        value = keyval[:, HEAD:].astype(jnp.bfloat16)
        for j in range(GROUP // 2):
            pair = jnp.dot(
                normed[...], wq[:, j * 256 : (j + 1) * 256], preferred_element_type=jnp.float32
            )
            for k in range(2):
                h = 2 * j + k
                queries[h * MICRO : (h + 1) * MICRO, :] = rotate(
                    pair[:, k * HEAD : (k + 1) * HEAD]
                ).astype(jnp.bfloat16)
        scores = lax.dot_general(
            queries[...], key, (((1,), (1,)), ((), ())), preferred_element_type=jnp.float32
        )
        ok = causal & (keyok[pl.ds(pl.multiple_of(i * 8, 8), 8), :][0:1, :] > 0.5)
        scores = (scores * score_scale).reshape(GROUP, MICRO, MICRO)
        scores = jnp.where(ok[None], scores, -jnp.inf)
        highest = jnp.max(scores, axis=-1, keepdims=True)
        weights = jnp.exp(scores - highest)
        total = jnp.sum(weights, axis=-1, keepdims=True)
        probs = (weights / total).astype(jnp.bfloat16).reshape(GROUP * MICRO, MICRO)
        mixed = jnp.dot(probs, value, preferred_element_type=jnp.float32).astype(jnp.bfloat16)
        for h in range(GROUP):
            context[:, h * HEAD : (h + 1) * HEAD] = mixed[h * MICRO : (h + 1) * MICRO, :]

        def project(half, j):
            start = pl.multiple_of(half * HALF + j * 256, 256)
            return lax.dot_general(
                context[...],
                wo[pl.ds(start, 256), :],
                (((1,), (1,)), ((), ())),
                preferred_element_type=jnp.float32,
            ).astype(jnp.bfloat16)

        for j in range(HALF // 256):
            psend[rows, j * 256 : (j + 1) * 256] = project(other, j)
        handed = give(i)
        handed.start()
        for j in range(HALF // 256):
            updated[rows, j * 256 : (j + 1) * 256] = project(core, j)
        handed.wait_recv()
        mine = updated[rows, :].astype(jnp.float32) + precv[rows, :].astype(jnp.float32)
        result = (stream[rows, own_cols].astype(jnp.float32) + mine).astype(jnp.bfloat16)
        updated[rows, :] = result

        @pl.when(section < SECTIONS - 1)
        def _():
            hop(i, section + 1).start()

        @pl.when(section == SECTIONS - 1)
        def _():
            kept = jnp.where(rowok[rows, :][:, 0:1] > 0.5, result, jnp.zeros_like(result))
            final[pl.ds(i * MFILES, MFILES)] = kept.reshape(MFILES, 2, 16, HALF)
            for target in range(SECTIONS - 1):
                src, dst = spread(i, target)
                pltpu.make_async_remote_copy(
                    src_ref=src,
                    dst_ref=dst,
                    send_sem=ssend.at[i, target],
                    recv_sem=srecv.at[i],
                    device_id=(dp, target, core),
                    device_id_type=MESH,
                ).start()
            src, dst = spread(i, SECTIONS - 1)
            pltpu.make_async_copy(src, dst, srecv.at[i]).start()

        return carry

    lax.fori_loop(0, MICROS, step, 0)

    def drain(i, carry):
        swap(i).wait_send()
        give(i).wait_send()

        @pl.when(section < SECTIONS - 1)
        def _():
            hop(i, section).wait_send()

        @pl.when(section == SECTIONS - 1)
        def _():
            for target in range(SECTIONS - 1):
                src, dst = spread(i, target)
                pltpu.make_async_copy(src, dst, ssend.at[i, target]).wait()

        files = piece.at[pl.ds(i * MFILES, MFILES), :, :]
        pltpu.make_async_copy(files, files, srecv.at[i]).wait()
        return carry

    lax.fori_loop(0, MICROS, drain, 0)
    out[...] = piece[...]


def per_device(hidden, lengths, dest_group, w_query, w_keyval, w_output, norm_gain, norm_bias):
    dp_count = lax.axis_size("dp")
    section_count = lax.axis_size("section")
    source_files, length_n, half_width = hidden.shape
    capacity = 2
    order = jnp.arange(source_files)
    earlier = (dest_group[None, :] == dest_group[:, None]) & (order[None, :] < order[:, None])
    position = jnp.sum(earlier.astype(jnp.int32), axis=1)
    hits = (
        (dest_group[None, None, :] == jnp.arange(dp_count)[:, None, None])
        & (position[None, None, :] == jnp.arange(capacity)[None, :, None])
    ).astype(jnp.int32)
    filled = jnp.sum(hits, axis=2)
    arrived_filled = lax.all_to_all(filled, "dp", split_axis=0, concat_axis=0, tiled=True)
    present = arrived_filled.reshape(-1)
    ranking = jnp.cumsum(present) - 1
    select = ((ranking[None, :] == jnp.arange(GSLOTS)[:, None]) & (present[None, :] > 0)).astype(
        jnp.bfloat16
    )

    inside = (jnp.arange(length_n)[None, :] < lengths[:, None]).astype(jnp.float32)
    keyok = jnp.broadcast_to(inside.reshape(MICROS, 1, MICRO), (MICROS, 8, MICRO)).reshape(
        MICROS * 8, MICRO
    )
    rowok = jnp.broadcast_to(inside.reshape(ROWS, 1), (ROWS, 128))
    cosine, sine = rope_tables(length_n, HEAD)
    cosine, sine = jnp.tile(cosine, (MFILES, 1)), jnp.tile(sine, (MFILES, 1))

    anywhere = pl.BlockSpec(memory_space=pl.ANY)
    inner = pl.BlockSpec(memory_space=pltpu.VMEM)
    dma = pltpu.SemaphoreType.DMA
    bf16 = jnp.bfloat16
    pieces = pl.pallas_call(
        layer_pipeline,
        out_shape=jax.ShapeDtypeStruct((FILES_N, 16, CUT), bf16),
        in_specs=[anywhere] * 4 + [inner] * 6,
        out_specs=inner,
        scratch_shapes=[
            pltpu.VMEM((WIDTH, HALF), bf16),
            pltpu.VMEM((WIDTH, HALF), bf16),
            pltpu.VMEM((WIDTH, 2 * HEAD), bf16),
            pltpu.VMEM((ROWS, WIDTH), bf16),
            pltpu.VMEM((ROWS, HALF), bf16),
            pltpu.VMEM((ROWS, HALF), bf16),
            pltpu.VMEM((ROWS, HALF), bf16),
            pltpu.VMEM((FILES_N, 2, 16, HALF), bf16),
            pltpu.VMEM((FILES_N, 16, CUT), bf16),
            pltpu.VMEM((MICRO, WIDTH), bf16),
            pltpu.VMEM((GROUP * MICRO, HEAD), bf16),
            pltpu.VMEM((MICRO, HALF), bf16),
            dma((4,)),
            dma((2, 4)),
            dma((2, 16, 4)),
            dma((MICROS,)),
            dma((MICROS,)),
            dma((MICROS,)),
            dma((MICROS,)),
            dma((MICROS,)),
            dma((MICROS,)),
            dma((MICROS, SECTIONS)),
            dma((MICROS,)),
        ],
        compiler_params=pltpu.CompilerParams(
            collective_id=0, has_side_effects=True, vmem_limit_bytes=56 * 2**20
        ),
        name="layers",
    )(
        hidden.reshape(ROWS, HALF),
        w_query[0],
        w_output[0],
        w_keyval[0].reshape(WIDTH, 2 * HEAD),
        norm_gain,
        norm_bias,
        cosine,
        sine,
        keyok,
        rowok,
    )
    flat = pieces.reshape(source_files, 16 * CUT)
    outgoing = jnp.dot(
        hits.reshape(dp_count * capacity, source_files).astype(bf16),
        flat,
        preferred_element_type=bf16,
    ).reshape(dp_count, capacity, 16 * CUT)
    arrived = lax.all_to_all(outgoing, "dp", split_axis=0, concat_axis=0, tiled=True)
    slots = jnp.dot(
        select, arrived.reshape(dp_count * capacity, 16 * CUT), preferred_element_type=bf16
    ).reshape(section_count, GSLOTS // section_count, 16 * CUT)
    mine = lax.all_to_all(slots, "section", split_axis=0, concat_axis=0, tiled=True)
    mine = mine.reshape(2, 4, 2, 16, CUT).transpose(2, 0, 3, 1, 4)
    return mine.reshape(GSLOTS // section_count, length_n, half_width)


def solution(mesh):
    in_specs = (
        P("dp", None, "mp"),
        P("dp"),
        P("dp"),
        P("section", "dp", "mp"),
        P("section", None, "mp", None, None),
        P("section", "dp", "mp"),
        P("section", None),
        P("section", None),
    )
    out_specs = P(("dp", "section"), None, "mp")
    return jax.shard_map(
        per_device, mesh=mesh, in_specs=in_specs, out_specs=out_specs, check_vma=False
    )
```

```python
import jax
import jax.numpy as jnp
import numpy as np
from jax import lax
from jax.experimental import pallas as pl
from jax.experimental.pallas import tpu as pltpu
from jax.sharding import PartitionSpec as P

GSLOTS = 16
MESH = pl.DeviceIdType.MESH

rope_base = 100000.0
norm_eps = 1e-05

FILES_N = 8
LEN = 32
ROWS = FILES_N * LEN
WIDTH = 3072
HALF = 1536
SHARD = 192
PART = 48
HEAD = 128
GROUP = 12
MICRO = 64
MICROS = ROWS // MICRO
MFILES = MICRO // LEN
SECTIONS = 8
SIDE = 4
CUT = 384
CHUNK = 512
CHUNKS = HALF // CHUNK
PLANE = SIDE * SIDE


def rope_tables(length_n, head_size):
    position = np.arange(length_n, dtype=np.float32)
    fraction = np.arange(head_size // 2, dtype=np.float32) * np.float32(2.0 / head_size)
    inverse = np.power(np.float32(rope_base), -fraction)
    angles = position[:, None] * inverse[None, :]
    cosine, sine = np.cos(angles), np.sin(angles)
    return (
        np.concatenate([cosine, cosine], axis=-1),
        np.concatenate([-sine, sine], axis=-1),
    )


def layer_pipeline(
    hidden, wq_own, wo_own, wkv_hbm, gain, bias, cosine, sine, dest_wide, dest_own, lengths, out,
    wq, wo, wkv, wot, stream, psend, precv, updated, final, piece, normed, queries, context,
    dest_all, outgoing, arrived_files, slots, landed, dest_s, slot_s,
    local_sem, gsend, grecv, zsend, zrecv, asend, arecv, rsend, rrecv, ssend, srecv,
    isend, irecv, fsend, frecv, osend, orecv,
):
    dp = lax.axis_index("dp")
    section = lax.axis_index("section")
    core = lax.axis_index("mp")
    x = lax.rem(dp, SIDE)
    y = dp // SIDE

    def at_xy(xx, yy):
        return lax.rem(yy + SIDE, SIDE) * SIDE + lax.rem(xx + SIDE, SIDE)

    other = 1 - core
    partner = (dp, section, other)
    steps = ((1, 0), (-1, 0), (0, 1), (0, -1))

    barrier = pltpu.get_barrier_semaphore()

    def greet(k, carry):
        pl.semaphore_signal(
            barrier,
            inc=1,
            device_id=(lax.rem(dp + k, PLANE), section, core),
            device_id_type=MESH,
        )
        return carry

    lax.fori_loop(1, PLANE, greet, 0)
    pl.semaphore_signal(barrier, inc=1, device_id=partner, device_id_type=MESH)
    for k in range(1, SECTIONS):
        pl.semaphore_signal(
            barrier, inc=1, device_id=(dp, lax.rem(section + k, SECTIONS), core), device_id_type=MESH
        )
    pl.semaphore_wait(barrier, PLANE - 1 + 1 + SECTIONS - 1)

    own_cols = pl.ds(pl.multiple_of(core * HALF, HALF), HALF)

    copies = [
        pltpu.make_async_copy(wq_own, wq.at[pl.ds(pl.multiple_of(dp * SHARD, SHARD), SHARD), :], local_sem.at[0]),
        pltpu.make_async_copy(wo_own, wo.at[pl.ds(pl.multiple_of(dp * SHARD, SHARD), SHARD), :], local_sem.at[1]),
        pltpu.make_async_copy(wkv_hbm, wkv, local_sem.at[2]),
    ]
    for copy in copies:
        copy.start()

    def rows_of(source, part):
        return pl.ds(pl.multiple_of(source * SHARD + part * PART, PART), PART)

    def push(w, source, part, direction, own):
        full = (wq, wo)[w]
        sx, sy = steps[direction]
        place = full.at[rows_of(source, part), :]
        src = (wq_own, wo_own)[w].at[pl.ds(part * PART, PART), :] if own else place
        pltpu.make_async_remote_copy(
            src_ref=src,
            dst_ref=place,
            send_sem=gsend.at[w, direction],
            recv_sem=grecv.at[w, source, part],
            device_id=(at_xy(x + sx, y + sy), section, core),
            device_id_type=MESH,
        ).start()

    def arrived(w, source, part):
        place = (wq, wo)[w].at[rows_of(source, part), :]
        pltpu.make_async_copy(place, place, grecv.at[w, source, part]).wait()

    def first_dirs(colour):
        return (0, 1) if colour == 0 else (2, 3)

    def second_dirs(colour):
        return (2, 3) if colour == 0 else (0, 1)

    def along(colour, k):
        return at_xy(x + k, y) if colour == 0 else at_xy(x, y + k)

    def across(colour, k, j):
        return at_xy(x + k, y + j) if colour == 0 else at_xy(x + j, y + k)

    def spread_own(w):
        for dirs in (first_dirs, second_dirs):
            for part in range(2):
                for colour in range(2):
                    for direction in dirs(colour):
                        push(w, dp, 2 * colour + part, direction, True)

    def relay_first(w):
        for part in range(2):
            for colour in range(2):
                forward, backward = first_dirs(colour)
                arrived(w, along(colour, -1), 2 * colour + part)
                if part == 0:
                    push(w, along(colour, -1), 2 * colour, forward, False)
                arrived(w, along(colour, 1), 2 * colour + part)
                if part == 1:
                    push(w, along(colour, 1), 2 * colour + 1, backward, False)
        for k in (-1, 1):
            for part in range(2):
                for colour in range(2):
                    for direction in second_dirs(colour):
                        push(w, along(colour, k), 2 * colour + part, direction, False)

    def relay_opposite(w):
        for part in range(2):
            for colour in range(2):
                arrived(w, along(colour, 2), 2 * colour + part)
                for direction in second_dirs(colour):
                    push(w, along(colour, 2), 2 * colour + part, direction, False)

    def relay_second(w, k):
        for part in range(2):
            for colour in range(2):
                forward, backward = second_dirs(colour)
                arrived(w, across(colour, k, -1), 2 * colour + part)
                if part == 0:
                    push(w, across(colour, k, -1), 2 * colour, forward, False)
                arrived(w, across(colour, k, 1), 2 * colour + part)
                if part == 1:
                    push(w, across(colour, k, 1), 2 * colour + 1, backward, False)

    def finish(w):
        for k in (0, -1, 1, 2):
            for part in range(2):
                for colour in range(2):
                    arrived(w, across(colour, k, 2), 2 * colour + part)

    def micro_rows(i):
        return pl.ds(pl.multiple_of(i * MICRO, MICRO), MICRO)

    def chunk_cols(j):
        return pl.ds(pl.multiple_of(core * HALF + j * CHUNK, CHUNK), CHUNK)

    def half_chunk(j):
        return pl.ds(j * CHUNK, CHUNK)

    def hop(i, j, to_section):
        rows = micro_rows(i)
        return pltpu.make_async_remote_copy(
            src_ref=updated.at[rows, half_chunk(j)],
            dst_ref=stream.at[rows, chunk_cols(j)],
            send_sem=zsend.at[i, j],
            recv_sem=zrecv.at[i, j],
            device_id=(dp, to_section, core),
            device_id_type=MESH,
        )

    def swap(i, j):
        rows = micro_rows(i)
        return pltpu.make_async_remote_copy(
            src_ref=stream.at[rows, chunk_cols(j)],
            dst_ref=stream.at[rows, chunk_cols(j)],
            send_sem=asend.at[i, j],
            recv_sem=arecv.at[i, j],
            device_id=partner,
            device_id_type=MESH,
        )

    def give(i, j):
        rows = micro_rows(i)
        return pltpu.make_async_remote_copy(
            src_ref=psend.at[rows, half_chunk(j)],
            dst_ref=precv.at[rows, half_chunk(j)],
            send_sem=rsend.at[i, j],
            recv_sem=rrecv.at[i, j],
            device_id=partner,
            device_id_type=MESH,
        )

    def spread(i, target):
        files = pl.ds(i * MFILES, MFILES)
        return (
            final.at[files, target // 4, :, pl.ds((target % 4) * CUT, CUT)],
            piece.at[files, :, :],
        )

    row_id = lax.broadcasted_iota(jnp.int32, (MICRO, MICRO), 0)
    col_id = lax.broadcasted_iota(jnp.int32, (MICRO, MICRO), 1)
    causal = (row_id // LEN == col_id // LEN) & (col_id <= row_id)
    score_scale = HEAD ** (-0.5)

    def inside(ids, i):
        limit = jnp.zeros_like(ids)
        for f in range(MFILES):
            limit = jnp.where(ids // LEN == f, lengths[i * MFILES + f] + f * LEN, limit)
        return ids < limit

    def attend(i):
        rows = micro_rows(i)
        for block in range(MICRO // 16):
            part = pl.ds(pl.multiple_of(i * MICRO + block * 16, 16), 16)
            values = stream[part, :].astype(jnp.float32)
            center = jnp.mean(values, axis=-1, keepdims=True)
            values = values - center
            variance = jnp.mean(values * values, axis=-1, keepdims=True)
            scaled = values * lax.rsqrt(variance + norm_eps)
            normed[block * 16 : (block + 1) * 16, :] = (scaled * gain[...] + bias[...]).astype(
                jnp.bfloat16
            )

        cos_t = cosine[...]
        sin_t = sine[...]

        def rotate(values):
            return values * cos_t + pltpu.roll(values, HEAD // 2, 1) * sin_t

        keyval = jnp.dot(normed[...], wkv[...], preferred_element_type=jnp.float32)
        key = rotate(keyval[:, :HEAD]).astype(jnp.bfloat16)
        value = keyval[:, HEAD:].astype(jnp.bfloat16)
        for j in range(GROUP // 2):
            pair = jnp.dot(
                normed[...], wq[:, j * 256 : (j + 1) * 256], preferred_element_type=jnp.float32
            )
            for k in range(2):
                h = 2 * j + k
                queries[h * MICRO : (h + 1) * MICRO, :] = rotate(
                    pair[:, k * HEAD : (k + 1) * HEAD]
                ).astype(jnp.bfloat16)
        scores = lax.dot_general(
            queries[...], key, (((1,), (1,)), ((), ())), preferred_element_type=jnp.float32
        )
        ok = causal & inside(col_id, i)
        scores = (scores * score_scale).reshape(GROUP, MICRO, MICRO)
        scores = jnp.where(ok[None], scores, -jnp.inf)
        highest = jnp.max(scores, axis=-1, keepdims=True)
        weights = jnp.exp(scores - highest)
        total = jnp.sum(weights, axis=-1, keepdims=True)
        probs = (weights / total).astype(jnp.bfloat16).reshape(GROUP * MICRO, MICRO)
        mixed = jnp.dot(probs, value, preferred_element_type=jnp.float32).astype(jnp.bfloat16)
        for h in range(GROUP):
            context[rows, h * HEAD : (h + 1) * HEAD] = mixed[h * MICRO : (h + 1) * MICRO, :]

    def project(i, half, j, turned):
        start = pl.multiple_of(half * HALF + j * 256, 256)
        if turned:
            return jnp.dot(
                context[micro_rows(i), :],
                wot[:, pl.ds(start, 256)],
                preferred_element_type=jnp.float32,
            ).astype(jnp.bfloat16)
        return lax.dot_general(
            context[micro_rows(i), :],
            wo[pl.ds(start, 256), :],
            (((1,), (1,)), ((), ())),
            preferred_element_type=jnp.float32,
        ).astype(jnp.bfloat16)

    def output(i, turned, last):
        rows = micro_rows(i)

        def others(c):
            for j in range(c * CHUNK // 256, (c + 1) * CHUNK // 256):
                psend[rows, j * 256 : (j + 1) * 256] = project(i, other, j, turned)
            give(i, c).start()

        def mine(c):
            for j in range(c * CHUNK // 256, (c + 1) * CHUNK // 256):
                updated[rows, j * 256 : (j + 1) * 256] = project(i, core, j, turned)

        def join(c):
            give(i, c).wait_recv()
            cols = half_chunk(c)
            total = updated[rows, cols].astype(jnp.float32) + precv[rows, cols].astype(jnp.float32)
            result = (stream[rows, chunk_cols(c)].astype(jnp.float32) + total).astype(jnp.bfloat16)
            updated[rows, cols] = result
            hop_on(c, result)

        def hop_on(c, result):
            if last is None:
                hop(i, c, section + 1).start()
            else:
                last(i, c, result)

        others(0)
        others(1)
        mine(0)
        others(2)
        join(0)
        mine(1)
        join(1)
        mine(2)
        join(2)

    def hold(i, c, result):
        @pl.when(section < SECTIONS - 1)
        def _():
            hop(i, c, section + 1).start()

        @pl.when(section == SECTIONS - 1)
        def _():
            kept = jnp.where(inside(row_id[:, 0:1], i), result, jnp.zeros_like(result))
            final[pl.ds(i * MFILES, MFILES), :, :, c * CHUNK : (c + 1) * CHUNK] = kept.reshape(
                MFILES, 2, 16, CHUNK
            )

    spread_own(0)

    dest_all[dp] = dest_wide[...]

    def tell(k, carry):
        to = lax.rem(dp + k, PLANE)
        pltpu.make_async_remote_copy(
            src_ref=dest_wide,
            dst_ref=dest_all.at[dp],
            send_sem=isend.at[0],
            recv_sem=irecv.at[0],
            device_id=(to, section, core),
            device_id_type=MESH,
        ).start()
        return carry

    lax.fori_loop(1, PLANE, tell, 0)

    @pl.when(section == 0)
    def _():
        first = pltpu.make_async_copy(hidden, stream.at[:, own_cols], local_sem.at[3])
        first.start()
        first.wait()

        def begin(i, carry):
            for j in range(CHUNKS):
                swap(i, j).start()
            return carry

        lax.fori_loop(0, MICROS, begin, 0)

    relay_first(0)
    spread_own(1)

    told = dest_all.at[pl.ds(0, PLANE - 1)]
    pltpu.make_async_copy(told, told, isend.at[0]).wait()
    pltpu.make_async_copy(told, told, irecv.at[0]).wait()
    lift = pltpu.make_async_copy(dest_all, dest_s, local_sem.at[4])
    lift.start()

    relay_opposite(0)
    relay_second(0, 0)
    lift.wait()

    def rank(source, carry):
        count, places = carry
        own_count = jnp.int32(0)
        for f in range(FILES_N):
            hit = dest_s[source, f, 0] == dp
            spot = source * 2 + own_count
            places = tuple(
                jnp.where(hit & (count == k), spot, places[k]) for k in range(GSLOTS)
            )
            step_up = jnp.where(hit, 1, 0)
            count = count + step_up
            own_count = own_count + step_up
        return count, places

    count, places = lax.fori_loop(0, PLANE, rank, (jnp.int32(0), (jnp.int32(0),) * GSLOTS))
    for k in range(GSLOTS):
        slot_s[k] = places[k]
    slot_s[GSLOTS] = count

    relay_first(1)
    relay_second(0, -1)
    relay_second(0, 1)
    relay_opposite(1)
    relay_second(0, 2)
    finish(0)
    for copy in copies:
        copy.wait()

    def relay_and_attend(t, carry):
        relay_second(1, jnp.where(t < 2, t, 5 - t))

        @pl.when(section == 0)
        def _():
            for j in range(CHUNKS):
                swap(t, j).wait_recv()
            attend(t)

        return carry

    lax.fori_loop(0, MICROS, relay_and_attend, 0)
    finish(1)

    @pl.when(section > 0)
    def _():
        def turn(j, carry):
            start = pl.multiple_of(j * 256, 256)
            wot[:, pl.ds(start, 256)] = wo[pl.ds(start, 256), :].T
            return carry

        lax.fori_loop(0, WIDTH // 256, turn, 0)

    def step(i, carry):
        @pl.when(section == 0)
        def _():
            output(i, False, None)

        @pl.when(section > 0)
        def _():
            for j in range(CHUNKS):
                hop(i, j, section).wait_recv()
                swap(i, j).start()
            for j in range(CHUNKS):
                swap(i, j).wait_recv()
            attend(i)
            output(i, True, hold)

        @pl.when(section == SECTIONS - 1)
        def _():
            for target in range(SECTIONS - 1):
                src, dst = spread(i, target)
                pltpu.make_async_remote_copy(
                    src_ref=src,
                    dst_ref=dst,
                    send_sem=ssend.at[i, target],
                    recv_sem=srecv.at[i],
                    device_id=(dp, target, core),
                    device_id_type=MESH,
                ).start()
            src, dst = spread(i, SECTIONS - 1)
            pltpu.make_async_copy(src, dst, srecv.at[i]).start()

        return carry

    lax.fori_loop(0, MICROS, step, 0)

    def gathered(i, carry):
        files = piece.at[pl.ds(i * MFILES, MFILES), :, :]
        pltpu.make_async_copy(files, files, srecv.at[i]).wait()
        return carry

    lax.fori_loop(0, MICROS, gathered, 0)

    def post(k, carry):
        to = lax.rem(dp + k, PLANE)
        picks = [jnp.int32(0), jnp.int32(0)]
        seen = jnp.int32(0)
        for f in range(FILES_N):
            hit = dest_own[f] == to
            for n in range(2):
                picks[n] = jnp.where(hit & (seen == n), f, picks[n])
            seen = seen + jnp.where(hit, 1, 0)
        for n in range(2):
            outgoing[2 * k + n] = piece[picks[n]]
        pair = outgoing.at[pl.ds(2 * k, 2)]
        land = arrived_files.at[pl.ds(2 * dp, 2)]

        @pl.when(k > 0)
        def _():
            pltpu.make_async_remote_copy(
                src_ref=pair,
                dst_ref=land,
                send_sem=fsend.at[0],
                recv_sem=frecv.at[0],
                device_id=(to, section, core),
                device_id_type=MESH,
            ).start()

        return carry

    lax.fori_loop(0, PLANE, post, 0)
    own_pair = pltpu.make_async_copy(
        outgoing.at[pl.ds(0, 2)], arrived_files.at[pl.ds(2 * dp, 2)], local_sem.at[5]
    )
    own_pair.start()
    own_pair.wait()
    posted = outgoing.at[pl.ds(0, 2 * (PLANE - 1))]
    pltpu.make_async_copy(posted, posted, frecv.at[0]).wait()

    for k in range(GSLOTS):
        block = arrived_files[slot_s[k]]
        slots[k] = jnp.where(k < slot_s[GSLOTS], block, jnp.zeros_like(block))

    def landing():
        return landed.at[:, section // 4, :, pl.ds(pl.multiple_of((section % 4) * CUT, CUT), CUT)]

    def deliver(k, carry):
        to = lax.rem(section + k, SECTIONS)
        pltpu.make_async_remote_copy(
            src_ref=slots.at[pl.ds(2 * to, 2)],
            dst_ref=landing(),
            send_sem=osend.at[0],
            recv_sem=orecv.at[0],
            device_id=(dp, to, core),
            device_id_type=MESH,
        ).start()
        return carry

    lax.fori_loop(1, SECTIONS, deliver, 0)
    own_slots = pltpu.make_async_copy(slots.at[pl.ds(2 * section, 2)], landing(), local_sem.at[5])
    own_slots.start()
    own_slots.wait()
    delivered = slots.at[pl.ds(0, 2 * (SECTIONS - 1))]
    pltpu.make_async_copy(delivered, delivered, orecv.at[0]).wait()
    out[...] = landed[...]

    def drain(i, carry):
        for j in range(CHUNKS):
            swap(i, j).wait_send()
            give(i, j).wait_send()

        @pl.when(section < SECTIONS - 1)
        def _():
            for j in range(CHUNKS):
                hop(i, j, section).wait_send()

        @pl.when(section == SECTIONS - 1)
        def _():
            for target in range(SECTIONS - 1):
                src, dst = spread(i, target)
                pltpu.make_async_copy(src, dst, ssend.at[i, target]).wait()

        return carry

    lax.fori_loop(0, MICROS, drain, 0)
    for w in range(2):
        for direction in range(4):
            sent = (wq, wo)[w].at[pl.ds(0, 15 * PART), :]
            pltpu.make_async_copy(sent, sent, gsend.at[w, direction]).wait()
    pltpu.make_async_copy(posted, posted, fsend.at[0]).wait()
    pltpu.make_async_copy(delivered, delivered, osend.at[0]).wait()


def per_device(hidden, lengths, dest_group, w_query, w_keyval, w_output, norm_gain, norm_bias):
    source_files, length_n, half_width = hidden.shape
    cosine, sine = rope_tables(length_n, HEAD)
    cosine, sine = jnp.asarray(np.tile(cosine, (MFILES, 1))), jnp.asarray(np.tile(sine, (MFILES, 1)))
    dest_wide = jnp.broadcast_to(dest_group[:, None], (source_files, 128))

    anywhere = pl.BlockSpec(memory_space=pl.ANY)
    inner = pl.BlockSpec(memory_space=pltpu.VMEM)
    scalar = pl.BlockSpec(memory_space=pltpu.SMEM)
    dma = pltpu.SemaphoreType.DMA
    bf16 = jnp.bfloat16
    rows = pl.pallas_call(
        layer_pipeline,
        out_shape=jax.ShapeDtypeStruct((2, 2, 16, HALF), bf16),
        in_specs=[anywhere] * 4 + [inner] * 5 + [scalar] * 2,
        out_specs=inner,
        scratch_shapes=[
            pltpu.VMEM((WIDTH, HALF), bf16),
            pltpu.VMEM((WIDTH, HALF), bf16),
            pltpu.VMEM((WIDTH, 2 * HEAD), bf16),
            pltpu.VMEM((HALF, WIDTH), bf16),
            pltpu.VMEM((ROWS, WIDTH), bf16),
            pltpu.VMEM((ROWS, HALF), bf16),
            pltpu.VMEM((ROWS, HALF), bf16),
            pltpu.VMEM((ROWS, HALF), bf16),
            pltpu.VMEM((FILES_N, 2, 16, HALF), bf16),
            pltpu.VMEM((FILES_N, 16, CUT), bf16),
            pltpu.VMEM((MICRO, WIDTH), bf16),
            pltpu.VMEM((GROUP * MICRO, HEAD), bf16),
            pltpu.VMEM((ROWS, HALF), bf16),
            pltpu.VMEM((PLANE, FILES_N, 128), jnp.int32),
            pltpu.VMEM((2 * PLANE, 16, CUT), bf16),
            pltpu.VMEM((2 * PLANE, 16, CUT), bf16),
            pltpu.VMEM((GSLOTS, 16, CUT), bf16),
            pltpu.VMEM((2, 2, 16, HALF), bf16),
            pltpu.SMEM((PLANE, FILES_N, 128), jnp.int32),
            pltpu.SMEM((GSLOTS + 1,), jnp.int32),
            dma((6,)),
            dma((2, 4)),
            dma((2, 16, 4)),
            dma((MICROS, CHUNKS)),
            dma((MICROS, CHUNKS)),
            dma((MICROS, CHUNKS)),
            dma((MICROS, CHUNKS)),
            dma((MICROS, CHUNKS)),
            dma((MICROS, CHUNKS)),
            dma((MICROS, SECTIONS)),
            dma((MICROS,)),
            dma((1,)),
            dma((1,)),
            dma((1,)),
            dma((1,)),
            dma((1,)),
            dma((1,)),
        ],
        compiler_params=pltpu.CompilerParams(
            collective_id=0, has_side_effects=True, vmem_limit_bytes=58 * 2**20
        ),
        name="layers",
    )(
        hidden.reshape(ROWS, HALF),
        w_query[0],
        w_output[0],
        w_keyval[0].reshape(WIDTH, 2 * HEAD),
        norm_gain,
        norm_bias,
        cosine,
        sine,
        dest_wide,
        dest_group,
        lengths,
    )
    return rows.reshape(GSLOTS // SECTIONS, length_n, half_width)


def solution(mesh):
    in_specs = (
        P("dp", None, "mp"),
        P("dp"),
        P("dp"),
        P("section", "dp", "mp"),
        P("section", None, "mp", None, None),
        P("section", "dp", "mp"),
        P("section", None),
        P("section", None),
    )
    out_specs = P(("dp", "section"), None, "mp")
    return jax.shard_map(
        per_device, mesh=mesh, in_specs=in_specs, out_specs=out_specs, check_vma=False
    )
```

```python
import jax
import jax.numpy as jnp
import numpy as np
from jax import lax
from jax.experimental import pallas as pl
from jax.experimental.pallas import tpu as pltpu
from jax.sharding import PartitionSpec as P

GSLOTS = 16
MESH = pl.DeviceIdType.MESH

rope_base = 100000.0
norm_eps = 1e-05

FILES_N = 8
LEN = 32
ROWS = FILES_N * LEN
WIDTH = 3072
HALF = 1536
SHARD = 192
PART = 48
HEAD = 128
GROUP = 12
MICRO = 64
MICROS = ROWS // MICRO
MFILES = MICRO // LEN
SECTIONS = 8
SIDE = 4
CUT = 384
CHUNK = 512
CHUNKS = HALF // CHUNK
PLANE = SIDE * SIDE


def rope_tables(length_n, head_size):
    position = np.arange(length_n, dtype=np.float32)
    fraction = np.arange(head_size // 2, dtype=np.float32) * np.float32(2.0 / head_size)
    inverse = np.power(np.float32(rope_base), -fraction)
    angles = position[:, None] * inverse[None, :]
    cosine, sine = np.cos(angles), np.sin(angles)
    return (
        np.concatenate([cosine, cosine], axis=-1),
        np.concatenate([-sine, sine], axis=-1),
    )


def layer_pipeline(
    hidden, wq_own, wo_own, wkv_hbm, gain, bias, cosine, sine, dest_wide, dest_own, lengths, out,
    wq, wo, wkv, wot, stream, psend, precv, updated, final, piece, normed, queries, context,
    dest_all, outgoing, arrived_files, slots, landed, dest_s, slot_s,
    local_sem, gsend, grecv, zsend, zrecv, asend, arecv, rsend, rrecv, ssend, srecv,
    isend, irecv, fsend, frecv, osend, orecv,
):
    dp = lax.axis_index("dp")
    section = lax.axis_index("section")
    core = lax.axis_index("mp")
    x = lax.rem(dp, SIDE)
    y = dp // SIDE

    def at_xy(xx, yy):
        return lax.rem(yy + SIDE, SIDE) * SIDE + lax.rem(xx + SIDE, SIDE)

    other = 1 - core
    partner = (dp, section, other)
    steps = ((1, 0), (-1, 0), (0, 1), (0, -1))

    barrier = pltpu.get_barrier_semaphore()

    def greet(k, carry):
        pl.semaphore_signal(
            barrier,
            inc=1,
            device_id=(lax.rem(dp + k, PLANE), section, core),
            device_id_type=MESH,
        )
        return carry

    lax.fori_loop(1, PLANE, greet, 0)
    pl.semaphore_signal(barrier, inc=1, device_id=partner, device_id_type=MESH)
    for k in range(1, SECTIONS):
        pl.semaphore_signal(
            barrier, inc=1, device_id=(dp, lax.rem(section + k, SECTIONS), core), device_id_type=MESH
        )
    pl.semaphore_wait(barrier, PLANE - 1 + 1 + SECTIONS - 1)

    own_cols = pl.ds(pl.multiple_of(core * HALF, HALF), HALF)

    copies = [
        pltpu.make_async_copy(wq_own, wq.at[pl.ds(pl.multiple_of(dp * SHARD, SHARD), SHARD), :], local_sem.at[0]),
        pltpu.make_async_copy(wo_own, wo.at[pl.ds(pl.multiple_of(dp * SHARD, SHARD), SHARD), :], local_sem.at[1]),
        pltpu.make_async_copy(wkv_hbm, wkv, local_sem.at[2]),
    ]
    for copy in copies:
        copy.start()

    def rows_of(source, part):
        return pl.ds(pl.multiple_of(source * SHARD + part * PART, PART), PART)

    def push(w, source, part, direction, own):
        full = (wq, wo)[w]
        sx, sy = steps[direction]
        place = full.at[rows_of(source, part), :]
        src = (wq_own, wo_own)[w].at[pl.ds(part * PART, PART), :] if own else place
        pltpu.make_async_remote_copy(
            src_ref=src,
            dst_ref=place,
            send_sem=gsend.at[w, direction],
            recv_sem=grecv.at[w, source, part],
            device_id=(at_xy(x + sx, y + sy), section, core),
            device_id_type=MESH,
        ).start()

    def arrived(w, source, part):
        place = (wq, wo)[w].at[rows_of(source, part), :]
        pltpu.make_async_copy(place, place, grecv.at[w, source, part]).wait()

    def first_dirs(colour):
        return (0, 1) if colour == 0 else (2, 3)

    def second_dirs(colour):
        return (2, 3) if colour == 0 else (0, 1)

    def along(colour, k):
        return at_xy(x + k, y) if colour == 0 else at_xy(x, y + k)

    def across(colour, k, j):
        return at_xy(x + k, y + j) if colour == 0 else at_xy(x + j, y + k)

    def spread_own(w):
        for dirs in (first_dirs, second_dirs):
            for part in range(2):
                for colour in range(2):
                    for direction in dirs(colour):
                        push(w, dp, 2 * colour + part, direction, True)

    def relay_first(w):
        for part in range(2):
            for colour in range(2):
                forward, backward = first_dirs(colour)
                arrived(w, along(colour, -1), 2 * colour + part)
                if part == 0:
                    push(w, along(colour, -1), 2 * colour, forward, False)
                arrived(w, along(colour, 1), 2 * colour + part)
                if part == 1:
                    push(w, along(colour, 1), 2 * colour + 1, backward, False)
        for k in (-1, 1):
            for part in range(2):
                for colour in range(2):
                    for direction in second_dirs(colour):
                        push(w, along(colour, k), 2 * colour + part, direction, False)

    def relay_opposite(w):
        for part in range(2):
            for colour in range(2):
                arrived(w, along(colour, 2), 2 * colour + part)
                for direction in second_dirs(colour):
                    push(w, along(colour, 2), 2 * colour + part, direction, False)

    def relay_second(w, k):
        for part in range(2):
            for colour in range(2):
                forward, backward = second_dirs(colour)
                arrived(w, across(colour, k, -1), 2 * colour + part)
                if part == 0:
                    push(w, across(colour, k, -1), 2 * colour, forward, False)
                arrived(w, across(colour, k, 1), 2 * colour + part)
                if part == 1:
                    push(w, across(colour, k, 1), 2 * colour + 1, backward, False)

    def finish(w):
        for k in (0, -1, 1, 2):
            for part in range(2):
                for colour in range(2):
                    arrived(w, across(colour, k, 2), 2 * colour + part)

    def micro_rows(i):
        return pl.ds(pl.multiple_of(i * MICRO, MICRO), MICRO)

    def chunk_cols(j):
        return pl.ds(pl.multiple_of(core * HALF + j * CHUNK, CHUNK), CHUNK)

    def half_chunk(j):
        return pl.ds(j * CHUNK, CHUNK)

    def hop(i, j, to_section):
        rows = micro_rows(i)
        return pltpu.make_async_remote_copy(
            src_ref=updated.at[rows, half_chunk(j)],
            dst_ref=stream.at[rows, chunk_cols(j)],
            send_sem=zsend.at[i, j],
            recv_sem=zrecv.at[i, j],
            device_id=(dp, to_section, core),
            device_id_type=MESH,
        )

    def swap(i, j):
        rows = micro_rows(i)
        return pltpu.make_async_remote_copy(
            src_ref=stream.at[rows, chunk_cols(j)],
            dst_ref=stream.at[rows, chunk_cols(j)],
            send_sem=asend.at[i, j],
            recv_sem=arecv.at[i, j],
            device_id=partner,
            device_id_type=MESH,
        )

    def give(i, j):
        rows = micro_rows(i)
        return pltpu.make_async_remote_copy(
            src_ref=psend.at[rows, half_chunk(j)],
            dst_ref=precv.at[rows, half_chunk(j)],
            send_sem=rsend.at[i, j],
            recv_sem=rrecv.at[i, j],
            device_id=partner,
            device_id_type=MESH,
        )

    def spread(i, target):
        files = pl.ds(i * MFILES, MFILES)
        return (
            final.at[files, target // 4, :, pl.ds((target % 4) * CUT, CUT)],
            piece.at[files, :, :],
        )

    row_id = lax.broadcasted_iota(jnp.int32, (MICRO, MICRO), 0)
    col_id = lax.broadcasted_iota(jnp.int32, (MICRO, MICRO), 1)
    causal = (row_id // LEN == col_id // LEN) & (col_id <= row_id)
    score_scale = HEAD ** (-0.5)

    def inside(ids, i):
        limit = jnp.zeros_like(ids)
        for f in range(MFILES):
            limit = jnp.where(ids // LEN == f, lengths[i * MFILES + f] + f * LEN, limit)
        return ids < limit

    def attend(i):
        rows = micro_rows(i)
        for block in range(MICRO // 16):
            part = pl.ds(pl.multiple_of(i * MICRO + block * 16, 16), 16)
            values = stream[part, :].astype(jnp.float32)
            center = jnp.mean(values, axis=-1, keepdims=True)
            values = values - center
            variance = jnp.mean(values * values, axis=-1, keepdims=True)
            scaled = values * lax.rsqrt(variance + norm_eps)
            normed[block * 16 : (block + 1) * 16, :] = (scaled * gain[...] + bias[...]).astype(
                jnp.bfloat16
            )

        cos_t = cosine[...]
        sin_t = sine[...]

        def rotate(values):
            return values * cos_t + pltpu.roll(values, HEAD // 2, 1) * sin_t

        keyval = jnp.dot(normed[...], wkv[...], preferred_element_type=jnp.float32)
        key = rotate(keyval[:, :HEAD]).astype(jnp.bfloat16)
        value = keyval[:, HEAD:].astype(jnp.bfloat16)
        for j in range(GROUP // 2):
            pair = jnp.dot(
                normed[...], wq[:, j * 256 : (j + 1) * 256], preferred_element_type=jnp.float32
            )
            for k in range(2):
                h = 2 * j + k
                queries[h * MICRO : (h + 1) * MICRO, :] = rotate(
                    pair[:, k * HEAD : (k + 1) * HEAD]
                ).astype(jnp.bfloat16)
        scores = lax.dot_general(
            queries[...], key, (((1,), (1,)), ((), ())), preferred_element_type=jnp.float32
        )
        ok = causal & inside(col_id, i)
        scores = (scores * score_scale).reshape(GROUP, MICRO, MICRO)
        scores = jnp.where(ok[None], scores, -jnp.inf)
        highest = jnp.max(scores, axis=-1, keepdims=True)
        weights = jnp.exp(scores - highest)
        total = jnp.sum(weights, axis=-1, keepdims=True)
        probs = (weights / total).astype(jnp.bfloat16).reshape(GROUP * MICRO, MICRO)
        mixed = jnp.dot(probs, value, preferred_element_type=jnp.float32).astype(jnp.bfloat16)
        for h in range(GROUP):
            context[rows, h * HEAD : (h + 1) * HEAD] = mixed[h * MICRO : (h + 1) * MICRO, :]

    def project(i, half, j, turned):
        start = pl.multiple_of(half * HALF + j * 256, 256)
        if turned:
            return jnp.dot(
                context[micro_rows(i), :],
                wot[:, pl.ds(start, 256)],
                preferred_element_type=jnp.float32,
            ).astype(jnp.bfloat16)
        return lax.dot_general(
            context[micro_rows(i), :],
            wo[pl.ds(start, 256), :],
            (((1,), (1,)), ((), ())),
            preferred_element_type=jnp.float32,
        ).astype(jnp.bfloat16)

    def fetch(i, j):
        hop(i, j, section).wait_recv()
        swap(i, j).start()

    def output(i, turned, last):
        rows = micro_rows(i)

        def ahead(chunks):
            if last is not None:

                @pl.when(i < MICROS - 1)
                def _():
                    for j in chunks:
                        fetch(i + 1, j)

        def others(c):
            for j in range(c * CHUNK // 256, (c + 1) * CHUNK // 256):
                psend[rows, j * 256 : (j + 1) * 256] = project(i, other, j, turned)
            give(i, c).start()

        def mine(c):
            for j in range(c * CHUNK // 256, (c + 1) * CHUNK // 256):
                updated[rows, j * 256 : (j + 1) * 256] = project(i, core, j, turned)

        def join(c):
            give(i, c).wait_recv()
            cols = half_chunk(c)
            total = updated[rows, cols].astype(jnp.float32) + precv[rows, cols].astype(jnp.float32)
            result = (stream[rows, chunk_cols(c)].astype(jnp.float32) + total).astype(jnp.bfloat16)
            updated[rows, cols] = result
            hop_on(c, result)

        def hop_on(c, result):
            if last is None:
                hop(i, c, section + 1).start()
            else:
                last(i, c, result)

        others(0)
        others(1)
        mine(0)
        others(2)
        join(0)
        mine(1)
        join(1)
        mine(2)
        ahead((0, 1))
        join(2)
        ahead((2,))

    def hold(i, c, result):
        @pl.when(section < SECTIONS - 1)
        def _():
            hop(i, c, section + 1).start()

        @pl.when(section == SECTIONS - 1)
        def _():
            kept = jnp.where(inside(row_id[:, 0:1], i), result, jnp.zeros_like(result))
            final[pl.ds(i * MFILES, MFILES), :, :, c * CHUNK : (c + 1) * CHUNK] = kept.reshape(
                MFILES, 2, 16, CHUNK
            )

    spread_own(0)

    dest_all[dp] = dest_wide[...]

    def tell(k, carry):
        to = lax.rem(dp + k, PLANE)
        pltpu.make_async_remote_copy(
            src_ref=dest_wide,
            dst_ref=dest_all.at[dp],
            send_sem=isend.at[0],
            recv_sem=irecv.at[0],
            device_id=(to, section, core),
            device_id_type=MESH,
        ).start()
        return carry

    lax.fori_loop(1, PLANE, tell, 0)

    @pl.when(section == 0)
    def _():
        first = pltpu.make_async_copy(hidden, stream.at[:, own_cols], local_sem.at[3])
        first.start()
        first.wait()

        def begin(i, carry):
            for j in range(CHUNKS):
                swap(i, j).start()
            return carry

        lax.fori_loop(0, MICROS, begin, 0)

    relay_first(0)
    spread_own(1)

    told = dest_all.at[pl.ds(0, PLANE - 1)]
    pltpu.make_async_copy(told, told, isend.at[0]).wait()
    pltpu.make_async_copy(told, told, irecv.at[0]).wait()
    lift = pltpu.make_async_copy(dest_all, dest_s, local_sem.at[4])
    lift.start()

    relay_opposite(0)
    relay_second(0, 0)
    lift.wait()

    def rank(source, carry):
        count, places = carry
        own_count = jnp.int32(0)
        for f in range(FILES_N):
            hit = dest_s[source, f, 0] == dp
            spot = source * 2 + own_count
            places = tuple(
                jnp.where(hit & (count == k), spot, places[k]) for k in range(GSLOTS)
            )
            step_up = jnp.where(hit, 1, 0)
            count = count + step_up
            own_count = own_count + step_up
        return count, places

    count, places = lax.fori_loop(0, PLANE, rank, (jnp.int32(0), (jnp.int32(0),) * GSLOTS))
    for k in range(GSLOTS):
        slot_s[k] = places[k]
    slot_s[GSLOTS] = count

    relay_first(1)
    relay_second(0, -1)
    relay_second(0, 1)
    relay_opposite(1)
    relay_second(0, 2)
    finish(0)
    for copy in copies:
        copy.wait()

    def relay_and_attend(t, carry):
        relay_second(1, jnp.where(t < 2, t, 5 - t))

        @pl.when(section == 0)
        def _():
            def early(i, inner):
                for j in range(CHUNKS):
                    swap(i, j).wait_recv()
                attend(i)
                return inner

            lax.fori_loop(t * (MICROS // SIDE), (t + 1) * (MICROS // SIDE), early, 0)

        return carry

    lax.fori_loop(0, SIDE, relay_and_attend, 0)
    finish(1)

    @pl.when(section > 0)
    def _():
        def turn(j, carry):
            start = pl.multiple_of(j * 256, 256)
            wot[:, pl.ds(start, 256)] = wo[pl.ds(start, 256), :].T
            return carry

        lax.fori_loop(0, WIDTH // 256, turn, 0)
        for j in range(CHUNKS):
            fetch(0, j)

    def step(i, carry):
        @pl.when(section == 0)
        def _():
            output(i, False, None)

        @pl.when(section > 0)
        def _():
            for j in range(CHUNKS):
                swap(i, j).wait_recv()
            attend(i)
            output(i, True, hold)

        @pl.when(section == SECTIONS - 1)
        def _():
            for target in range(SECTIONS - 1):
                src, dst = spread(i, target)
                pltpu.make_async_remote_copy(
                    src_ref=src,
                    dst_ref=dst,
                    send_sem=ssend.at[i, target],
                    recv_sem=srecv.at[i],
                    device_id=(dp, target, core),
                    device_id_type=MESH,
                ).start()
            src, dst = spread(i, SECTIONS - 1)
            pltpu.make_async_copy(src, dst, srecv.at[i]).start()

        return carry

    lax.fori_loop(0, MICROS, step, 0)

    def gathered(i, carry):
        files = piece.at[pl.ds(i * MFILES, MFILES), :, :]
        pltpu.make_async_copy(files, files, srecv.at[i]).wait()
        return carry

    lax.fori_loop(0, MICROS, gathered, 0)

    def post(k, carry):
        to = lax.rem(dp + k, PLANE)
        picks = [jnp.int32(0), jnp.int32(0)]
        seen = jnp.int32(0)
        for f in range(FILES_N):
            hit = dest_own[f] == to
            for n in range(2):
                picks[n] = jnp.where(hit & (seen == n), f, picks[n])
            seen = seen + jnp.where(hit, 1, 0)
        for n in range(2):
            outgoing[2 * k + n] = piece[picks[n]]
        pair = outgoing.at[pl.ds(2 * k, 2)]
        land = arrived_files.at[pl.ds(2 * dp, 2)]

        @pl.when(k > 0)
        def _():
            pltpu.make_async_remote_copy(
                src_ref=pair,
                dst_ref=land,
                send_sem=fsend.at[0],
                recv_sem=frecv.at[0],
                device_id=(to, section, core),
                device_id_type=MESH,
            ).start()

        return carry

    lax.fori_loop(0, PLANE, post, 0)
    own_pair = pltpu.make_async_copy(
        outgoing.at[pl.ds(0, 2)], arrived_files.at[pl.ds(2 * dp, 2)], local_sem.at[5]
    )
    own_pair.start()
    own_pair.wait()
    posted = outgoing.at[pl.ds(0, 2 * (PLANE - 1))]
    pltpu.make_async_copy(posted, posted, frecv.at[0]).wait()

    for k in range(GSLOTS):
        block = arrived_files[slot_s[k]]
        slots[k] = jnp.where(k < slot_s[GSLOTS], block, jnp.zeros_like(block))

    def landing():
        return landed.at[:, section // 4, :, pl.ds(pl.multiple_of((section % 4) * CUT, CUT), CUT)]

    def deliver(k, carry):
        to = lax.rem(section + k, SECTIONS)
        pltpu.make_async_remote_copy(
            src_ref=slots.at[pl.ds(2 * to, 2)],
            dst_ref=landing(),
            send_sem=osend.at[0],
            recv_sem=orecv.at[0],
            device_id=(dp, to, core),
            device_id_type=MESH,
        ).start()
        return carry

    lax.fori_loop(1, SECTIONS, deliver, 0)
    own_slots = pltpu.make_async_copy(slots.at[pl.ds(2 * section, 2)], landing(), local_sem.at[5])
    own_slots.start()
    own_slots.wait()
    delivered = slots.at[pl.ds(0, 2 * (SECTIONS - 1))]
    pltpu.make_async_copy(delivered, delivered, orecv.at[0]).wait()
    out[...] = landed[...]

    def drain(i, carry):
        for j in range(CHUNKS):
            swap(i, j).wait_send()
            give(i, j).wait_send()

        @pl.when(section < SECTIONS - 1)
        def _():
            for j in range(CHUNKS):
                hop(i, j, section).wait_send()

        @pl.when(section == SECTIONS - 1)
        def _():
            for target in range(SECTIONS - 1):
                src, dst = spread(i, target)
                pltpu.make_async_copy(src, dst, ssend.at[i, target]).wait()

        return carry

    lax.fori_loop(0, MICROS, drain, 0)
    for w in range(2):
        for direction in range(4):
            sent = (wq, wo)[w].at[pl.ds(0, 15 * PART), :]
            pltpu.make_async_copy(sent, sent, gsend.at[w, direction]).wait()
    pltpu.make_async_copy(posted, posted, fsend.at[0]).wait()
    pltpu.make_async_copy(delivered, delivered, osend.at[0]).wait()


def per_device(hidden, lengths, dest_group, w_query, w_keyval, w_output, norm_gain, norm_bias):
    source_files, length_n, half_width = hidden.shape
    cosine, sine = rope_tables(length_n, HEAD)
    cosine, sine = jnp.asarray(np.tile(cosine, (MFILES, 1))), jnp.asarray(np.tile(sine, (MFILES, 1)))
    dest_wide = jnp.broadcast_to(dest_group[:, None], (source_files, 128))

    anywhere = pl.BlockSpec(memory_space=pl.ANY)
    inner = pl.BlockSpec(memory_space=pltpu.VMEM)
    scalar = pl.BlockSpec(memory_space=pltpu.SMEM)
    dma = pltpu.SemaphoreType.DMA
    bf16 = jnp.bfloat16
    rows = pl.pallas_call(
        layer_pipeline,
        out_shape=jax.ShapeDtypeStruct((2, 2, 16, HALF), bf16),
        in_specs=[anywhere] * 4 + [inner] * 5 + [scalar] * 2,
        out_specs=inner,
        scratch_shapes=[
            pltpu.VMEM((WIDTH, HALF), bf16),
            pltpu.VMEM((WIDTH, HALF), bf16),
            pltpu.VMEM((WIDTH, 2 * HEAD), bf16),
            pltpu.VMEM((HALF, WIDTH), bf16),
            pltpu.VMEM((ROWS, WIDTH), bf16),
            pltpu.VMEM((ROWS, HALF), bf16),
            pltpu.VMEM((ROWS, HALF), bf16),
            pltpu.VMEM((ROWS, HALF), bf16),
            pltpu.VMEM((FILES_N, 2, 16, HALF), bf16),
            pltpu.VMEM((FILES_N, 16, CUT), bf16),
            pltpu.VMEM((MICRO, WIDTH), bf16),
            pltpu.VMEM((GROUP * MICRO, HEAD), bf16),
            pltpu.VMEM((ROWS, HALF), bf16),
            pltpu.VMEM((PLANE, FILES_N, 128), jnp.int32),
            pltpu.VMEM((2 * PLANE, 16, CUT), bf16),
            pltpu.VMEM((2 * PLANE, 16, CUT), bf16),
            pltpu.VMEM((GSLOTS, 16, CUT), bf16),
            pltpu.VMEM((2, 2, 16, HALF), bf16),
            pltpu.SMEM((PLANE, FILES_N, 128), jnp.int32),
            pltpu.SMEM((GSLOTS + 1,), jnp.int32),
            dma((6,)),
            dma((2, 4)),
            dma((2, 16, 4)),
            dma((MICROS, CHUNKS)),
            dma((MICROS, CHUNKS)),
            dma((MICROS, CHUNKS)),
            dma((MICROS, CHUNKS)),
            dma((MICROS, CHUNKS)),
            dma((MICROS, CHUNKS)),
            dma((MICROS, SECTIONS)),
            dma((MICROS,)),
            dma((1,)),
            dma((1,)),
            dma((1,)),
            dma((1,)),
            dma((1,)),
            dma((1,)),
        ],
        compiler_params=pltpu.CompilerParams(
            collective_id=0, has_side_effects=True, vmem_limit_bytes=58 * 2**20
        ),
        name="layers",
    )(
        hidden.reshape(ROWS, HALF),
        w_query[0],
        w_output[0],
        w_keyval[0].reshape(WIDTH, 2 * HEAD),
        norm_gain,
        norm_bias,
        cosine,
        sine,
        dest_wide,
        dest_group,
        lengths,
    )
    return rows.reshape(GSLOTS // SECTIONS, length_n, half_width)


def solution(mesh):
    in_specs = (
        P("dp", None, "mp"),
        P("dp"),
        P("dp"),
        P("section", "dp", "mp"),
        P("section", None, "mp", None, None),
        P("section", "dp", "mp"),
        P("section", None),
        P("section", None),
    )
    out_specs = P(("dp", "section"), None, "mp")
    return jax.shard_map(
        per_device, mesh=mesh, in_specs=in_specs, out_specs=out_specs, check_vma=False
    )
```

```python
import jax
import jax.numpy as jnp
import numpy as np
from jax import lax
from jax.experimental import pallas as pl
from jax.experimental.pallas import tpu as pltpu
from jax.sharding import PartitionSpec as P

GSLOTS = 16
MESH = pl.DeviceIdType.MESH

rope_base = 100000.0
norm_eps = 1e-05

FILES_N = 8
LEN = 32
ROWS = FILES_N * LEN
WIDTH = 3072
HALF = 1536
SHARD = 192
PART = 48
HEAD = 128
GROUP = 12
MICRO = 32
MICROS = ROWS // MICRO
MFILES = MICRO // LEN
SECTIONS = 8
SIDE = 4
CUT = 384
CHUNK = 512
CHUNKS = HALF // CHUNK
PLANE = SIDE * SIDE


def rope_tables(length_n, head_size):
    position = np.arange(length_n, dtype=np.float32)
    fraction = np.arange(head_size // 2, dtype=np.float32) * np.float32(2.0 / head_size)
    inverse = np.power(np.float32(rope_base), -fraction)
    angles = position[:, None] * inverse[None, :]
    cosine, sine = np.cos(angles), np.sin(angles)
    return (
        np.concatenate([cosine, cosine], axis=-1),
        np.concatenate([-sine, sine], axis=-1),
    )


def layer_pipeline(
    hidden, wq_own, wo_own, wkv_hbm, gain, bias, cosine, sine, dest_wide, dest_own, lengths, out,
    wq, wo, wkv, wot, stream, psend, precv, updated, final, piece, normed, queries, context,
    dest_all, outgoing, arrived_files, slots, landed, dest_s, slot_s,
    local_sem, gsend, grecv, zsend, zrecv, asend, arecv, rsend, rrecv, ssend, srecv,
    isend, irecv, fsend, frecv, osend, orecv,
):
    dp = lax.axis_index("dp")
    section = lax.axis_index("section")
    core = lax.axis_index("mp")
    x = lax.rem(dp, SIDE)
    y = dp // SIDE

    def at_xy(xx, yy):
        return lax.rem(yy + SIDE, SIDE) * SIDE + lax.rem(xx + SIDE, SIDE)

    other = 1 - core
    partner = (dp, section, other)
    steps = ((1, 0), (-1, 0), (0, 1), (0, -1))

    barrier = pltpu.get_barrier_semaphore()

    def greet(k, carry):
        pl.semaphore_signal(
            barrier,
            inc=1,
            device_id=(lax.rem(dp + k, PLANE), section, core),
            device_id_type=MESH,
        )
        return carry

    lax.fori_loop(1, PLANE, greet, 0)
    pl.semaphore_signal(barrier, inc=1, device_id=partner, device_id_type=MESH)
    for k in range(1, SECTIONS):
        pl.semaphore_signal(
            barrier, inc=1, device_id=(dp, lax.rem(section + k, SECTIONS), core), device_id_type=MESH
        )
    pl.semaphore_wait(barrier, PLANE - 1 + 1 + SECTIONS - 1)

    own_cols = pl.ds(pl.multiple_of(core * HALF, HALF), HALF)

    copies = [
        pltpu.make_async_copy(wq_own, wq.at[pl.ds(pl.multiple_of(dp * SHARD, SHARD), SHARD), :], local_sem.at[0]),
        pltpu.make_async_copy(wo_own, wo.at[pl.ds(pl.multiple_of(dp * SHARD, SHARD), SHARD), :], local_sem.at[1]),
        pltpu.make_async_copy(wkv_hbm, wkv, local_sem.at[2]),
    ]
    for copy in copies:
        copy.start()

    def rows_of(source, part):
        return pl.ds(pl.multiple_of(source * SHARD + part * PART, PART), PART)

    def push(w, source, part, direction, own):
        full = (wq, wo)[w]
        sx, sy = steps[direction]
        place = full.at[rows_of(source, part), :]
        src = (wq_own, wo_own)[w].at[pl.ds(part * PART, PART), :] if own else place
        pltpu.make_async_remote_copy(
            src_ref=src,
            dst_ref=place,
            send_sem=gsend.at[w, direction],
            recv_sem=grecv.at[w, source, part],
            device_id=(at_xy(x + sx, y + sy), section, core),
            device_id_type=MESH,
        ).start()

    def arrived(w, source, part):
        place = (wq, wo)[w].at[rows_of(source, part), :]
        pltpu.make_async_copy(place, place, grecv.at[w, source, part]).wait()

    def first_dirs(colour):
        return (0, 1) if colour == 0 else (2, 3)

    def second_dirs(colour):
        return (2, 3) if colour == 0 else (0, 1)

    def along(colour, k):
        return at_xy(x + k, y) if colour == 0 else at_xy(x, y + k)

    def across(colour, k, j):
        return at_xy(x + k, y + j) if colour == 0 else at_xy(x + j, y + k)

    def spread_own(w):
        for dirs in (first_dirs, second_dirs):
            for part in range(2):
                for colour in range(2):
                    for direction in dirs(colour):
                        push(w, dp, 2 * colour + part, direction, True)

    def relay_first(w):
        for part in range(2):
            for colour in range(2):
                forward, backward = first_dirs(colour)
                arrived(w, along(colour, -1), 2 * colour + part)
                if part == 0:
                    push(w, along(colour, -1), 2 * colour, forward, False)
                arrived(w, along(colour, 1), 2 * colour + part)
                if part == 1:
                    push(w, along(colour, 1), 2 * colour + 1, backward, False)
        for k in (-1, 1):
            for part in range(2):
                for colour in range(2):
                    for direction in second_dirs(colour):
                        push(w, along(colour, k), 2 * colour + part, direction, False)

    def relay_opposite(w):
        for part in range(2):
            for colour in range(2):
                arrived(w, along(colour, 2), 2 * colour + part)
                for direction in second_dirs(colour):
                    push(w, along(colour, 2), 2 * colour + part, direction, False)

    def relay_second(w, k):
        for part in range(2):
            for colour in range(2):
                forward, backward = second_dirs(colour)
                arrived(w, across(colour, k, -1), 2 * colour + part)
                if part == 0:
                    push(w, across(colour, k, -1), 2 * colour, forward, False)
                arrived(w, across(colour, k, 1), 2 * colour + part)
                if part == 1:
                    push(w, across(colour, k, 1), 2 * colour + 1, backward, False)

    def finish(w):
        for k in (0, -1, 1, 2):
            for part in range(2):
                for colour in range(2):
                    arrived(w, across(colour, k, 2), 2 * colour + part)

    def micro_rows(i):
        return pl.ds(pl.multiple_of(i * MICRO, MICRO), MICRO)

    def chunk_cols(j):
        return pl.ds(pl.multiple_of(core * HALF + j * CHUNK, CHUNK), CHUNK)

    def half_chunk(j):
        return pl.ds(j * CHUNK, CHUNK)

    def hop(i, j, to_section):
        rows = micro_rows(i)
        return pltpu.make_async_remote_copy(
            src_ref=updated.at[rows, half_chunk(j)],
            dst_ref=stream.at[rows, chunk_cols(j)],
            send_sem=zsend.at[i, j],
            recv_sem=zrecv.at[i, j],
            device_id=(dp, to_section, core),
            device_id_type=MESH,
        )

    def swap(i, j):
        rows = micro_rows(i)
        return pltpu.make_async_remote_copy(
            src_ref=stream.at[rows, chunk_cols(j)],
            dst_ref=stream.at[rows, chunk_cols(j)],
            send_sem=asend.at[i, j],
            recv_sem=arecv.at[i, j],
            device_id=partner,
            device_id_type=MESH,
        )

    def give(i, j):
        rows = micro_rows(i)
        return pltpu.make_async_remote_copy(
            src_ref=psend.at[rows, half_chunk(j)],
            dst_ref=precv.at[rows, half_chunk(j)],
            send_sem=rsend.at[i, j],
            recv_sem=rrecv.at[i, j],
            device_id=partner,
            device_id_type=MESH,
        )

    def spread(i, target):
        files = pl.ds(i * MFILES, MFILES)
        return (
            final.at[files, target // 4, :, pl.ds((target % 4) * CUT, CUT)],
            piece.at[files, :, :],
        )

    row_id = lax.broadcasted_iota(jnp.int32, (MICRO, MICRO), 0)
    col_id = lax.broadcasted_iota(jnp.int32, (MICRO, MICRO), 1)
    causal = (row_id // LEN == col_id // LEN) & (col_id <= row_id)
    score_scale = HEAD ** (-0.5)

    def inside(ids, i):
        limit = jnp.zeros_like(ids)
        for f in range(MFILES):
            limit = jnp.where(ids // LEN == f, lengths[i * MFILES + f] + f * LEN, limit)
        return ids < limit

    def attend(i):
        rows = micro_rows(i)
        for block in range(MICRO // 16):
            part = pl.ds(pl.multiple_of(i * MICRO + block * 16, 16), 16)
            values = stream[part, :].astype(jnp.float32)
            center = jnp.mean(values, axis=-1, keepdims=True)
            values = values - center
            variance = jnp.mean(values * values, axis=-1, keepdims=True)
            scaled = values * lax.rsqrt(variance + norm_eps)
            normed[block * 16 : (block + 1) * 16, :] = (scaled * gain[...] + bias[...]).astype(
                jnp.bfloat16
            )

        cos_t = cosine[...]
        sin_t = sine[...]

        def rotate(values):
            return values * cos_t + pltpu.roll(values, HEAD // 2, 1) * sin_t

        keyval = jnp.dot(normed[...], wkv[...], preferred_element_type=jnp.float32)
        key = rotate(keyval[:, :HEAD]).astype(jnp.bfloat16)
        value = keyval[:, HEAD:].astype(jnp.bfloat16)
        for j in range(GROUP // 2):
            pair = jnp.dot(
                normed[...], wq[:, j * 256 : (j + 1) * 256], preferred_element_type=jnp.float32
            )
            for k in range(2):
                h = 2 * j + k
                queries[h * MICRO : (h + 1) * MICRO, :] = rotate(
                    pair[:, k * HEAD : (k + 1) * HEAD]
                ).astype(jnp.bfloat16)
        scores = lax.dot_general(
            queries[...], key, (((1,), (1,)), ((), ())), preferred_element_type=jnp.float32
        )
        ok = causal & inside(col_id, i)
        scores = (scores * score_scale).reshape(GROUP, MICRO, MICRO)
        scores = jnp.where(ok[None], scores, -jnp.inf)
        highest = jnp.max(scores, axis=-1, keepdims=True)
        weights = jnp.exp(scores - highest)
        total = jnp.sum(weights, axis=-1, keepdims=True)
        probs = (weights / total).astype(jnp.bfloat16).reshape(GROUP * MICRO, MICRO)
        mixed = jnp.dot(probs, value, preferred_element_type=jnp.float32).astype(jnp.bfloat16)
        for h in range(GROUP):
            context[rows, h * HEAD : (h + 1) * HEAD] = mixed[h * MICRO : (h + 1) * MICRO, :]

    def project(i, half, j, turned):
        start = pl.multiple_of(half * HALF + j * 256, 256)
        if turned:
            return jnp.dot(
                context[micro_rows(i), :],
                wot[:, pl.ds(start, 256)],
                preferred_element_type=jnp.float32,
            ).astype(jnp.bfloat16)
        return lax.dot_general(
            context[micro_rows(i), :],
            wo[pl.ds(start, 256), :],
            (((1,), (1,)), ((), ())),
            preferred_element_type=jnp.float32,
        ).astype(jnp.bfloat16)

    def fetch(i, j):
        hop(i, j, section).wait_recv()
        swap(i, j).start()

    def output(i, turned, last):
        rows = micro_rows(i)

        def ahead(chunks):
            if last is not None:

                @pl.when(i < MICROS - 1)
                def _():
                    for j in chunks:
                        fetch(i + 1, j)

        def others(c):
            for j in range(c * CHUNK // 256, (c + 1) * CHUNK // 256):
                psend[rows, j * 256 : (j + 1) * 256] = project(i, other, j, turned)
            give(i, c).start()

        def mine(c):
            for j in range(c * CHUNK // 256, (c + 1) * CHUNK // 256):
                updated[rows, j * 256 : (j + 1) * 256] = project(i, core, j, turned)

        def join(c):
            give(i, c).wait_recv()
            cols = half_chunk(c)
            total = updated[rows, cols].astype(jnp.float32) + precv[rows, cols].astype(jnp.float32)
            result = (stream[rows, chunk_cols(c)].astype(jnp.float32) + total).astype(jnp.bfloat16)
            updated[rows, cols] = result
            hop_on(c, result)

        def hop_on(c, result):
            if last is None:
                hop(i, c, section + 1).start()
            else:
                last(i, c, result)

        others(0)
        others(1)
        mine(0)
        others(2)
        join(0)
        mine(1)
        join(1)
        mine(2)
        ahead((0, 1))
        join(2)
        ahead((2,))

    def hold(i, c, result):
        @pl.when(section < SECTIONS - 1)
        def _():
            hop(i, c, section + 1).start()

        @pl.when(section == SECTIONS - 1)
        def _():
            kept = jnp.where(inside(row_id[:, 0:1], i), result, jnp.zeros_like(result))
            final[pl.ds(i * MFILES, MFILES), :, :, c * CHUNK : (c + 1) * CHUNK] = kept.reshape(
                MFILES, 2, 16, CHUNK
            )

    spread_own(0)

    dest_all[dp] = dest_wide[...]

    def tell(k, carry):
        to = lax.rem(dp + k, PLANE)
        pltpu.make_async_remote_copy(
            src_ref=dest_wide,
            dst_ref=dest_all.at[dp],
            send_sem=isend.at[0],
            recv_sem=irecv.at[0],
            device_id=(to, section, core),
            device_id_type=MESH,
        ).start()
        return carry

    lax.fori_loop(1, PLANE, tell, 0)

    @pl.when(section == 0)
    def _():
        first = pltpu.make_async_copy(hidden, stream.at[:, own_cols], local_sem.at[3])
        first.start()
        first.wait()

        def begin(i, carry):
            for j in range(CHUNKS):
                swap(i, j).start()
            return carry

        lax.fori_loop(0, MICROS, begin, 0)

    relay_first(0)
    spread_own(1)

    told = dest_all.at[pl.ds(0, PLANE - 1)]
    pltpu.make_async_copy(told, told, isend.at[0]).wait()
    pltpu.make_async_copy(told, told, irecv.at[0]).wait()
    lift = pltpu.make_async_copy(dest_all, dest_s, local_sem.at[4])
    lift.start()

    relay_opposite(0)
    relay_second(0, 0)
    lift.wait()

    def rank(source, carry):
        count, places = carry
        own_count = jnp.int32(0)
        for f in range(FILES_N):
            hit = dest_s[source, f, 0] == dp
            spot = source * 2 + own_count
            places = tuple(
                jnp.where(hit & (count == k), spot, places[k]) for k in range(GSLOTS)
            )
            step_up = jnp.where(hit, 1, 0)
            count = count + step_up
            own_count = own_count + step_up
        return count, places

    count, places = lax.fori_loop(0, PLANE, rank, (jnp.int32(0), (jnp.int32(0),) * GSLOTS))
    for k in range(GSLOTS):
        slot_s[k] = places[k]
    slot_s[GSLOTS] = count

    relay_first(1)
    relay_second(0, -1)
    relay_second(0, 1)
    relay_opposite(1)
    relay_second(0, 2)
    finish(0)
    for copy in copies:
        copy.wait()

    def relay_and_attend(t, carry):
        relay_second(1, jnp.where(t < 2, t, 5 - t))

        @pl.when(section == 0)
        def _():
            def early(i, inner):
                for j in range(CHUNKS):
                    swap(i, j).wait_recv()
                attend(i)
                return inner

            lax.fori_loop(t * (MICROS // SIDE), (t + 1) * (MICROS // SIDE), early, 0)

        return carry

    lax.fori_loop(0, SIDE, relay_and_attend, 0)
    finish(1)

    @pl.when(section > 0)
    def _():
        def turn(j, carry):
            start = pl.multiple_of(j * 256, 256)
            wot[:, pl.ds(start, 256)] = wo[pl.ds(start, 256), :].T
            return carry

        lax.fori_loop(0, WIDTH // 256, turn, 0)
        for j in range(CHUNKS):
            fetch(0, j)

    def step(i, carry):
        @pl.when(section == 0)
        def _():
            output(i, False, None)

        @pl.when(section > 0)
        def _():
            for j in range(CHUNKS):
                swap(i, j).wait_recv()
            attend(i)
            output(i, True, hold)

        @pl.when(section == SECTIONS - 1)
        def _():
            for target in range(SECTIONS - 1):
                src, dst = spread(i, target)
                pltpu.make_async_remote_copy(
                    src_ref=src,
                    dst_ref=dst,
                    send_sem=ssend.at[i, target],
                    recv_sem=srecv.at[i],
                    device_id=(dp, target, core),
                    device_id_type=MESH,
                ).start()
            src, dst = spread(i, SECTIONS - 1)
            pltpu.make_async_copy(src, dst, srecv.at[i]).start()

        return carry

    lax.fori_loop(0, MICROS, step, 0)

    def gathered(i, carry):
        files = piece.at[pl.ds(i * MFILES, MFILES), :, :]
        pltpu.make_async_copy(files, files, srecv.at[i]).wait()
        return carry

    lax.fori_loop(0, MICROS, gathered, 0)

    def post(k, carry):
        to = lax.rem(dp + k, PLANE)
        picks = [jnp.int32(0), jnp.int32(0)]
        seen = jnp.int32(0)
        for f in range(FILES_N):
            hit = dest_own[f] == to
            for n in range(2):
                picks[n] = jnp.where(hit & (seen == n), f, picks[n])
            seen = seen + jnp.where(hit, 1, 0)
        for n in range(2):
            outgoing[2 * k + n] = piece[picks[n]]
        pair = outgoing.at[pl.ds(2 * k, 2)]
        land = arrived_files.at[pl.ds(2 * dp, 2)]

        @pl.when(k > 0)
        def _():
            pltpu.make_async_remote_copy(
                src_ref=pair,
                dst_ref=land,
                send_sem=fsend.at[0],
                recv_sem=frecv.at[0],
                device_id=(to, section, core),
                device_id_type=MESH,
            ).start()

        return carry

    lax.fori_loop(0, PLANE, post, 0)
    own_pair = pltpu.make_async_copy(
        outgoing.at[pl.ds(0, 2)], arrived_files.at[pl.ds(2 * dp, 2)], local_sem.at[5]
    )
    own_pair.start()
    own_pair.wait()
    posted = outgoing.at[pl.ds(0, 2 * (PLANE - 1))]
    pltpu.make_async_copy(posted, posted, frecv.at[0]).wait()

    for k in range(GSLOTS):
        block = arrived_files[slot_s[k]]
        slots[k] = jnp.where(k < slot_s[GSLOTS], block, jnp.zeros_like(block))

    def landing():
        return landed.at[:, section // 4, :, pl.ds(pl.multiple_of((section % 4) * CUT, CUT), CUT)]

    def deliver(k, carry):
        to = lax.rem(section + k, SECTIONS)
        pltpu.make_async_remote_copy(
            src_ref=slots.at[pl.ds(2 * to, 2)],
            dst_ref=landing(),
            send_sem=osend.at[0],
            recv_sem=orecv.at[0],
            device_id=(dp, to, core),
            device_id_type=MESH,
        ).start()
        return carry

    lax.fori_loop(1, SECTIONS, deliver, 0)
    own_slots = pltpu.make_async_copy(slots.at[pl.ds(2 * section, 2)], landing(), local_sem.at[5])
    own_slots.start()
    own_slots.wait()
    delivered = slots.at[pl.ds(0, 2 * (SECTIONS - 1))]
    pltpu.make_async_copy(delivered, delivered, orecv.at[0]).wait()
    out[...] = landed[...]

    def drain(i, carry):
        for j in range(CHUNKS):
            swap(i, j).wait_send()
            give(i, j).wait_send()

        @pl.when(section < SECTIONS - 1)
        def _():
            for j in range(CHUNKS):
                hop(i, j, section).wait_send()

        @pl.when(section == SECTIONS - 1)
        def _():
            for target in range(SECTIONS - 1):
                src, dst = spread(i, target)
                pltpu.make_async_copy(src, dst, ssend.at[i, target]).wait()

        return carry

    lax.fori_loop(0, MICROS, drain, 0)
    for w in range(2):
        for direction in range(4):
            sent = (wq, wo)[w].at[pl.ds(0, 15 * PART), :]
            pltpu.make_async_copy(sent, sent, gsend.at[w, direction]).wait()
    pltpu.make_async_copy(posted, posted, fsend.at[0]).wait()
    pltpu.make_async_copy(delivered, delivered, osend.at[0]).wait()


def per_device(hidden, lengths, dest_group, w_query, w_keyval, w_output, norm_gain, norm_bias):
    source_files, length_n, half_width = hidden.shape
    cosine, sine = rope_tables(length_n, HEAD)
    cosine, sine = jnp.asarray(np.tile(cosine, (MFILES, 1))), jnp.asarray(np.tile(sine, (MFILES, 1)))
    dest_wide = jnp.broadcast_to(dest_group[:, None], (source_files, 128))

    anywhere = pl.BlockSpec(memory_space=pl.ANY)
    inner = pl.BlockSpec(memory_space=pltpu.VMEM)
    scalar = pl.BlockSpec(memory_space=pltpu.SMEM)
    dma = pltpu.SemaphoreType.DMA
    bf16 = jnp.bfloat16
    rows = pl.pallas_call(
        layer_pipeline,
        out_shape=jax.ShapeDtypeStruct((2, 2, 16, HALF), bf16),
        in_specs=[anywhere] * 4 + [inner] * 5 + [scalar] * 2,
        out_specs=inner,
        scratch_shapes=[
            pltpu.VMEM((WIDTH, HALF), bf16),
            pltpu.VMEM((WIDTH, HALF), bf16),
            pltpu.VMEM((WIDTH, 2 * HEAD), bf16),
            pltpu.VMEM((HALF, WIDTH), bf16),
            pltpu.VMEM((ROWS, WIDTH), bf16),
            pltpu.VMEM((ROWS, HALF), bf16),
            pltpu.VMEM((ROWS, HALF), bf16),
            pltpu.VMEM((ROWS, HALF), bf16),
            pltpu.VMEM((FILES_N, 2, 16, HALF), bf16),
            pltpu.VMEM((FILES_N, 16, CUT), bf16),
            pltpu.VMEM((MICRO, WIDTH), bf16),
            pltpu.VMEM((GROUP * MICRO, HEAD), bf16),
            pltpu.VMEM((ROWS, HALF), bf16),
            pltpu.VMEM((PLANE, FILES_N, 128), jnp.int32),
            pltpu.VMEM((2 * PLANE, 16, CUT), bf16),
            pltpu.VMEM((2 * PLANE, 16, CUT), bf16),
            pltpu.VMEM((GSLOTS, 16, CUT), bf16),
            pltpu.VMEM((2, 2, 16, HALF), bf16),
            pltpu.SMEM((PLANE, FILES_N, 128), jnp.int32),
            pltpu.SMEM((GSLOTS + 1,), jnp.int32),
            dma((6,)),
            dma((2, 4)),
            dma((2, 16, 4)),
            dma((MICROS, CHUNKS)),
            dma((MICROS, CHUNKS)),
            dma((MICROS, CHUNKS)),
            dma((MICROS, CHUNKS)),
            dma((MICROS, CHUNKS)),
            dma((MICROS, CHUNKS)),
            dma((MICROS, SECTIONS)),
            dma((MICROS,)),
            dma((1,)),
            dma((1,)),
            dma((1,)),
            dma((1,)),
            dma((1,)),
            dma((1,)),
        ],
        compiler_params=pltpu.CompilerParams(
            collective_id=0, has_side_effects=True, vmem_limit_bytes=58 * 2**20
        ),
        name="layers",
    )(
        hidden.reshape(ROWS, HALF),
        w_query[0],
        w_output[0],
        w_keyval[0].reshape(WIDTH, 2 * HEAD),
        norm_gain,
        norm_bias,
        cosine,
        sine,
        dest_wide,
        dest_group,
        lengths,
    )
    return rows.reshape(GSLOTS // SECTIONS, length_n, half_width)


def solution(mesh):
    in_specs = (
        P("dp", None, "mp"),
        P("dp"),
        P("dp"),
        P("section", "dp", "mp"),
        P("section", None, "mp", None, None),
        P("section", "dp", "mp"),
        P("section", None),
        P("section", None),
    )
    out_specs = P(("dp", "section"), None, "mp")
    return jax.shard_map(
        per_device, mesh=mesh, in_specs=in_specs, out_specs=out_specs, check_vma=False
    )
```
